128 devices in a mesh: dp: 8 (over z, core), mem: 16 (over y, x).
Axes of the slice: x: 4, y: 4, z: 4, core: 2. Of those that a mesh axis runs over, the one named last changes fastest.
Arguments:
- tokens: bfloat16 [8, 3072, 2048], P('dp')
- w_query: bfloat16 [2048, 2048], P(None, 'mem'), may hold values from -0.125 to 0.125
- w_key: bfloat16 [2048, 2048], P(None, 'mem'), may hold values from -0.125 to 0.125
- w_value: bfloat16 [2048, 2048], P(None, 'mem'), may hold values from -0.125 to 0.125
- gate_bias: float32 [16], P('mem'), may hold values from -2 to 2
- memory_keys: bfloat16 [8, 24576, 2048], P('dp', 'mem')
- memory_values: bfloat16 [8, 24576, 2048], P('dp', 'mem'), may hold values from -6 to 6
- retrieval_ids: int32 [8, 16, 24, 8], P('dp', 'mem'), may hold values from 0 to 383, as said below
- retrieval_counts: int32 [8, 16, 24], P('dp', 'mem'), may hold values from 1 to 8, as said below
- cotangent: bfloat16 [8, 3072, 2048], P('dp', None, 'mem')
Outputs:
- attended: bfloat16 [8, 3072, 2048], P('dp', None, 'mem')
- grad_q: float32 [2048, 2048], P('dp', 'mem')
- grad_k: float32 [2048, 2048], P('dp', 'mem')
- grad_v: float32 [2048, 2048], P('dp', 'mem')
- grad_gate: float32 [16], P('mem')
The draws below stay inside these ranges and needn't reach their ends.
Inputs may be any that keep to these rules, and one draw needn't show every extreme that they name: `retrieval_ids`: entry [d, h, b, j] names tile t of document d's memory, owned by index t // 24 of mem; only entries j < retrieval_counts[d, h, b] are live, the others are padding with arbitrary tile ids. Over the live entries of one head at most 12 name tiles of one owner, and in each document one owner is named by exactly 12 live entries of every head. `retrieval_counts`: the number of leading live entries of the list of block b of head h.
All inputs are finite; a program needn't handle non-finite values.
Results may differ from the reference program's by a relative error of at most 0.011.
Values may be sent and summed in bfloat16 or wider, within the bound.
No kernel may reach another device: no remote copies, remote signals or barrier semaphores. Data moves between devices by JAX's collectives and lax.ppermute only.
A program may use at most 128 MiB of HBM per device.

```python
import jax
import jax.numpy as jnp
from jax import lax

D = 2048
HEADS = 16
DH = 128
SEG = 512
QB = 128
TILE = 64
TOP = 8
SEGS = 6
TILES_DEV = 24
DOCS = 8
TOK = 3072
NQB = 24
CAP = 12
MEM = 24576
TILES = 384


def retrieval_lists(key):
    base_key = jax.random.fold_in(key, 11)
    keys_all = jax.random.split(base_key, 8)
    slot_total = NQB * TOP
    owners_all = TILES // TILES_DEV
    spread = (owners_all - 1) * CAP
    hot_owner = jax.random.randint(keys_all[0], (DOCS, 1, 1), 0, owners_all)
    small_count = jax.random.randint(keys_all[1], (DOCS, HEADS, NQB), 1, 4)
    pick_full = jax.random.randint(keys_all[2], (DOCS, HEADS, NQB), 0, 4) == 0
    forced = jax.random.randint(keys_all[3], (DOCS, 1, 1), 0, HEADS * NQB)
    flat_index = jnp.arange(HEADS * NQB).reshape(1, HEADS, NQB)
    counts = jnp.where(pick_full | (flat_index == forced), TOP, small_count).astype(jnp.int32)
    live_slot = (jnp.arange(TOP)[None, None, None, :] < counts[..., None]).reshape(DOCS, HEADS, slot_total)
    order_score = jax.random.randint(keys_all[4], (DOCS, HEADS, slot_total), 0, slot_total) * slot_total + jnp.arange(slot_total)
    order_score = jnp.where(live_slot, order_score, order_score + slot_total * slot_total)
    slot_order = jnp.argsort(order_score, axis=-1, stable=True)
    position = jnp.argsort(slot_order, axis=-1, stable=True)
    spread_base = jnp.arange(spread)[None, None, :] // CAP
    other_owner = spread_base + (spread_base >= hot_owner).astype(jnp.int32)
    other_owner = jnp.broadcast_to(other_owner, (DOCS, HEADS, spread))
    mix_score = jax.random.randint(keys_all[5], (DOCS, HEADS, spread), 0, spread) * spread + jnp.arange(spread)
    mix_order = jnp.argsort(mix_score, axis=-1, stable=True)
    other_seq = jnp.take_along_axis(other_owner, mix_order, axis=-1)
    rest_index = jnp.clip(position - CAP, 0, spread - 1)
    rest_owner = jnp.take_along_axis(other_seq, rest_index, axis=-1)
    live_owner = jnp.where(position < CAP, hot_owner, rest_owner)
    pad_owner = jax.random.randint(keys_all[6], (DOCS, HEADS, slot_total), 0, owners_all)
    owner_id = jnp.where(live_slot, live_owner, pad_owner)
    local_tile = jax.random.randint(keys_all[7], (DOCS, HEADS, slot_total), 0, TILES_DEV)
    tile_ids = (owner_id * TILES_DEV + local_tile).reshape(DOCS, HEADS, NQB, TOP).astype(jnp.int32)
    return (tile_ids, counts)


def draw_retrieval_ids(key, part):
    return retrieval_lists(key)[0]


def draw_retrieval_counts(key, part):
    return retrieval_lists(key)[1]


def draw_tokens(key, part):
    shape_all = (DOCS, TOK, D)
    values = jax.random.normal(key, shape_all, jnp.float32)
    return values.astype(jnp.bfloat16)


def draw_memory_keys(key, part):
    shape_all = (DOCS, TILES, TILE, HEADS * DH)
    values = jax.random.normal(key, shape_all, jnp.float32)
    return values.reshape(DOCS, MEM, HEADS * DH).astype(jnp.bfloat16)


def draw_cotangent(key, part):
    shape_all = (DOCS, TOK, HEADS * DH)
    position = jnp.arange(DOCS, dtype=jnp.float32)[:, None, None] / (DOCS - 1)
    scaling = (DOCS * TOK) ** (-0.5)
    values = jax.random.normal(key, shape_all, jnp.float32) * (1.0 + 2.0 * position)
    return (values * scaling).astype(jnp.bfloat16)


def block_scale(rng, extent, pieces, low, high):
    gain = 1.0
    for axis_at, shards_of in pieces:
        draws = jax.random.uniform(jax.random.fold_in(jax.random.fold_in(rng, 6), axis_at), (shards_of,), jnp.float32, low / len(pieces), high / len(pieces))
        gain = gain * jnp.repeat(jnp.exp(draws), extent[axis_at] // shards_of).reshape((-1,) + (1,) * (len(extent) - 1 - axis_at))
    return gain


def bell_draw(rng, extent, scale, bound, cuts=(), held_as=jnp.bfloat16):
    array = jax.random.normal(rng, extent, jnp.float32) * scale
    if len(cuts) > 0:
        array = block_scale(rng, extent, cuts, -0.22, 0.18) * array
    return jnp.clip(array, min=-bound, max=bound).astype(held_as)


def setup_inputs(seed: int = 0) -> dict:
    streams_of = jax.random.split(jax.random.key(seed), 11)
    tokens = draw_tokens(jax.random.fold_in(streams_of[10], 71), 0)
    w_query = bell_draw(streams_of[1], (D, HEADS * DH), D ** -0.5, 0.125, ((1, 16),))
    w_key = bell_draw(streams_of[2], (D, HEADS * DH), D ** -0.5, 0.125, ((1, 16),))
    w_value = bell_draw(streams_of[3], (D, HEADS * DH), D ** -0.5, 0.125, ((1, 16),))
    gate_bias = jnp.clip(jax.random.uniform(streams_of[4], (HEADS,), jnp.float32, -2.0, 2.0) * block_scale(streams_of[4], (HEADS,), ((0, 16),), -0.4, 0.0), -2.0, 2.0)
    memory_keys = draw_memory_keys(jax.random.fold_in(streams_of[10], 71), 0)
    memory_values = bell_draw(streams_of[6], (DOCS, MEM, HEADS * DH), 1.0, 6.0, ((0, 8), (1, 16)))
    retrieval_ids = draw_retrieval_ids(jax.random.fold_in(streams_of[10], 71), 0)
    retrieval_counts = draw_retrieval_counts(jax.random.fold_in(streams_of[10], 71), 0)
    cotangent = draw_cotangent(jax.random.fold_in(streams_of[10], 71), 0)
    return {"tokens": tokens, "w_query": w_query, "w_key": w_key, "w_value": w_value, "gate_bias": gate_bias, "memory_keys": memory_keys, "memory_values": memory_values, "retrieval_ids": retrieval_ids, "retrieval_counts": retrieval_counts, "cotangent": cotangent}


def rounded(values):
    return lax.optimization_barrier(values.astype(jnp.bfloat16)).astype(jnp.float32)


def split_heads(matrix):
    return matrix.reshape(matrix.shape[0], HEADS, DH).transpose(1, 0, 2)


def join_heads(stacked):
    return stacked.transpose(1, 0, 2).reshape(stacked.shape[1], HEADS * DH)


def softmax_rows(scores):
    largest = jnp.max(scores, axis=-1, keepdims=True)
    raised = jnp.exp(scores - largest)
    return raised / jnp.sum(raised, axis=-1, keepdims=True)


def back_softmax(soft_rows, grad_rows, scaling):
    return soft_rows * (grad_rows - jnp.sum(grad_rows * soft_rows, axis=-1, keepdims=True)) * scaling


def reference(tokens, w_query, w_key, w_value, gate_bias, memory_keys, memory_values, retrieval_ids, retrieval_counts, cotangent):
    scaling = DH ** -0.5
    causal = jnp.arange(SEG)[:, None] >= jnp.arange(SEG)[None, :]
    gate = jax.nn.sigmoid(gate_bias.astype(jnp.float32))
    gate_col = gate[:, None, None]
    head_index = jnp.arange(HEADS)[:, None, None]

    def one_document(carry, inputs):
        hidden, mem_keys, mem_values, tile_ids, counts, upstream_in = inputs
        queries = split_heads(jnp.dot(hidden, w_query, preferred_element_type=jnp.float32).astype(jnp.bfloat16))
        keys_local = split_heads(jnp.dot(hidden, w_key, preferred_element_type=jnp.float32).astype(jnp.bfloat16))
        values_local = split_heads(jnp.dot(hidden, w_value, preferred_element_type=jnp.float32).astype(jnp.bfloat16))
        seg_queries = queries.reshape(HEADS, SEGS, SEG, DH).astype(jnp.float32)
        seg_keys = keys_local.reshape(HEADS, SEGS, SEG, DH).astype(jnp.float32)
        seg_values = values_local.reshape(HEADS, SEGS, SEG, DH).astype(jnp.float32)
        local_scores = jnp.einsum("hnqe,hnke->hnqk", seg_queries, seg_keys) * scaling
        local_probs = softmax_rows(jnp.where(causal, local_scores, -jnp.inf))
        local_round = rounded(local_probs)
        local_out = jnp.einsum("hnqk,hnke->hnqe", local_round, seg_values).reshape(HEADS, TOK, DH)
        key_tiles = mem_keys.reshape(TILES, TILE, HEADS, DH)[tile_ids, :, head_index]
        key_tiles = key_tiles.reshape(HEADS, NQB, TOP * TILE, DH).astype(jnp.float32)
        value_tiles = mem_values.reshape(TILES, TILE, HEADS, DH)[tile_ids, :, head_index]
        value_tiles = value_tiles.reshape(HEADS, NQB, TOP * TILE, DH).astype(jnp.float32)
        live_slot = jnp.arange(TOP)[None, None, :] < counts[:, :, None]
        live_keys = jnp.repeat(live_slot, TILE, axis=2)[:, :, None, :]
        block_queries = queries.reshape(HEADS, NQB, QB, DH).astype(jnp.float32)
        mem_scores = jnp.einsum("hbqe,hbke->hbqk", block_queries, key_tiles) * scaling
        mem_probs = softmax_rows(jnp.where(live_keys, mem_scores, -jnp.inf))
        mem_round = rounded(mem_probs)
        mem_out = jnp.einsum("hbqk,hbke->hbqe", mem_round, value_tiles).reshape(HEADS, TOK, DH)
        attended = join_heads((gate_col * mem_out + (1.0 - gate_col) * local_out).astype(jnp.bfloat16))
        upstream = split_heads(upstream_in).astype(jnp.float32)
        gate_term = jnp.sum(upstream * (mem_out - local_out), axis=(1, 2)) * gate * (1.0 - gate)
        grad_mem = rounded(gate_col * upstream)
        grad_local = rounded((1.0 - gate_col) * upstream)
        mem_grad_rows = jnp.einsum("hbqe,hbke->hbqk", grad_mem.reshape(HEADS, NQB, QB, DH), value_tiles)
        mem_dround = rounded(back_softmax(mem_probs, mem_grad_rows, scaling))
        mem_dq = jnp.einsum("hbqk,hbke->hbqe", mem_dround, key_tiles).reshape(HEADS, TOK, DH)
        seg_grad = grad_local.reshape(HEADS, SEGS, SEG, DH)
        local_grad_rows = jnp.einsum("hnqe,hnke->hnqk", seg_grad, seg_values)
        local_dround = rounded(back_softmax(local_probs, local_grad_rows, scaling))
        local_dq = jnp.einsum("hnqk,hnke->hnqe", local_dround, seg_keys).reshape(HEADS, TOK, DH)
        grad_queries = (mem_dq + local_dq).astype(jnp.bfloat16)
        grad_keys = jnp.einsum("hnqk,hnqe->hnke", local_dround, seg_queries).astype(jnp.bfloat16).reshape(HEADS, TOK, DH)
        grad_values = jnp.einsum("hnqk,hnqe->hnke", local_round, seg_grad).astype(jnp.bfloat16).reshape(HEADS, TOK, DH)
        weight_q = jnp.dot(hidden.T, join_heads(grad_queries), preferred_element_type=jnp.float32)
        weight_k = jnp.dot(hidden.T, join_heads(grad_keys), preferred_element_type=jnp.float32)
        weight_v = jnp.dot(hidden.T, join_heads(grad_values), preferred_element_type=jnp.float32)
        carry = (carry[0] + weight_q, carry[1] + weight_k, carry[2] + weight_v, carry[3] + gate_term)
        return carry, attended

    zero_weight = jnp.zeros((D, HEADS * DH), jnp.float32)
    start = (zero_weight, zero_weight, zero_weight, jnp.zeros((HEADS,), jnp.float32))
    totals, attended = lax.scan(one_document, start, (tokens, memory_keys, memory_values, retrieval_ids, retrieval_counts, cotangent))
    return (attended, totals[0], totals[1], totals[2], totals[3])
```

```python
import functools

import jax
import jax.numpy as jnp
from jax import lax
from jax.experimental import pallas as pl
from jax.experimental.pallas import tpu as pltpu
from jax.sharding import PartitionSpec as P

DH = 128
SEG = 512
QB = 128
TILE = 64
TOP = 8
SEGS = 6
TILES_DEV = 24
TOK = 3072
NQB = 24
CAP = 12
MEMS = 16
D = 2048
ENTRIES = NQB * TOP
SCALING = DH ** (-0.5)
ROWS_OUT = D // 8
GATE_ROWS = 16
F32 = jnp.float32
BF16 = jnp.bfloat16
MIB = 1 << 20

NT = (((1,), (1,)), ((), ()))
TN = (((0,), (0,)), ((), ()))


def dot(a, b, dims=(((1,), (0,)), ((), ()))):
    return lax.dot_general(a, b, dims, preferred_element_type=F32)


def iota(shape, dim):
    return lax.broadcasted_iota(jnp.int32, shape, dim)


def gate_row(bias_ref):
    return 1.0 / (1.0 + jnp.exp(-jnp.full((1, DH), bias_ref[0], F32)))


def request_kernel(ids_ref, counts_ref, table_ref, slot_ref):
    ids = ids_ref[...]
    owner = (ids // TILES_DEV).astype(F32)
    local = (ids % TILES_DEV).astype(F32)
    counts = counts_ref[...].astype(F32)
    by_block = (iota((ENTRIES, NQB), 0) // TOP == iota((ENTRIES, NQB), 1)).astype(F32)
    pick = (iota((ENTRIES, TOP), 0) % TOP == iota((ENTRIES, TOP), 1)).astype(F32)
    owner_col = jnp.sum(dot(by_block, owner) * pick, axis=1, keepdims=True)
    local_col = jnp.sum(dot(by_block, local) * pick, axis=1, keepdims=True)
    count_col = jnp.sum(by_block * counts, axis=1, keepdims=True)
    slot_col = (iota((ENTRIES, 1), 0) % TOP).astype(F32)
    owner_col = jnp.where(slot_col < count_col, owner_col, float(MEMS))
    of_block = (iota((NQB, ENTRIES), 1) // TOP == iota((NQB, ENTRIES), 0)).astype(F32)
    of_slot = (iota((TOP, ENTRIES), 1) % TOP == iota((TOP, ENTRIES), 0)).astype(F32)
    owner_row = jnp.sum(dot(owner, of_slot) * of_block, axis=0, keepdims=True)
    count_row = dot(jnp.broadcast_to(counts, (8, NQB)), of_block)[:1]
    slot_row = (iota((1, ENTRIES), 1) % TOP).astype(F32)
    owner_row = jnp.where(slot_row < count_row, owner_row, float(MEMS))
    same = owner_col == owner_row
    first = iota((ENTRIES, ENTRIES), 0)
    second = iota((ENTRIES, ENTRIES), 1)
    rank_col = jnp.sum((same & (second < first)).astype(F32), axis=1, keepdims=True)
    rank_row = jnp.sum((same & (first < second)).astype(F32), axis=0, keepdims=True)
    sends = (owner_row == iota((MEMS, ENTRIES), 0).astype(F32)).astype(F32)
    place = jnp.where(rank_col == iota((ENTRIES, 128), 1).astype(F32), local_col, 0.0)
    table_ref[...] = dot(sends, place).astype(jnp.int32)
    slot_ref[...] = jnp.clip(owner_row * CAP + rank_row, 0.0, float(MEMS * CAP - 1)).astype(jnp.int32)


def make_requests(ids, counts):
    return pl.pallas_call(
        request_kernel,
        out_shape=(
            jax.ShapeDtypeStruct((MEMS, 128), jnp.int32),
            jax.ShapeDtypeStruct((1, ENTRIES), jnp.int32),
        ),
        name="request",
    )(ids, counts)


def serve_kernel(wanted_ref, keys_ref, values_ref, out_ref, sem):
    def issue(i, _):
        dest = i // CAP
        rank = i % CAP
        rows = pl.ds(pl.multiple_of(wanted_ref[dest, rank] * TILE, TILE), TILE)
        cols = pl.ds(pl.multiple_of(dest * DH, DH), DH)
        pltpu.make_async_copy(keys_ref.at[rows, cols], out_ref.at[i, 0], sem).start()
        pltpu.make_async_copy(values_ref.at[rows, cols], out_ref.at[i, 1], sem).start()
        return 0

    lax.fori_loop(0, MEMS * CAP, issue, 0, unroll=4)
    pltpu.make_async_copy(out_ref, out_ref, sem).wait()


def serve(wanted, keys, values):
    hbm = pl.BlockSpec(memory_space=pl.ANY)
    return pl.pallas_call(
        serve_kernel,
        out_shape=jax.ShapeDtypeStruct((MEMS * CAP, 2, TILE, DH), BF16),
        in_specs=[pl.BlockSpec(memory_space=pltpu.SMEM), hbm, hbm],
        out_specs=hbm,
        scratch_shapes=[pltpu.SemaphoreType.DMA(())],
        cost_estimate=pl.CostEstimate(flops=0, bytes_accessed=12 * MIB, transcendentals=0),
        name="serve",
    )(wanted, keys, values)


def local_kernel(
    tokens_ref, wq_ref, wk_ref, wv_ref, cot_ref, bias_ref,
    queries_ref, out_ref, dq_ref, grad_ref, weights, total,
):
    step = pl.program_id(0)

    @pl.when(step == 0)
    def _():
        weights[:, :DH] = wq_ref[...]
        weights[:, DH : 2 * DH] = wk_ref[...]
        weights[:, 2 * DH :] = wv_ref[...]
        total[...] = jnp.zeros_like(total)

    x = tokens_ref[...]
    qkv = dot(x, weights[...]).astype(BF16)
    q, k, v = qkv[:, :DH], qkv[:, DH : 2 * DH], qkv[:, 2 * DH :]
    queries_ref[...] = q
    gate = gate_row(bias_ref)
    grad = ((1.0 - gate) * cot_ref[...].astype(F32)).astype(BF16)
    half = SEG // 2
    grad_k = []
    grad_v = []
    for part in range(2):
        rows = slice(part * half, (part + 1) * half)
        width = (part + 1) * half
        qs, gs, ks, vs = q[rows], grad[rows], k[:width], v[:width]
        scores = dot(qs, ks, NT) * SCALING
        keep = iota((half, width), 0) + part * half >= iota((half, width), 1)
        scores = jnp.where(keep, scores, -jnp.inf)
        raised = jnp.exp(scores - jnp.max(scores, axis=1, keepdims=True))
        probs = raised * (1.0 / jnp.sum(raised, axis=1, keepdims=True))
        rounded = probs.astype(BF16)
        out_ref[rows, :] = dot(rounded, vs)
        back = dot(gs, vs, NT)
        dscore = probs * (back - jnp.sum(back * probs, axis=1, keepdims=True)) * SCALING
        dround = dscore.astype(BF16)
        dq_ref[rows, :] = dot(dround, ks)
        grad_k.append(dot(dround, qs, TN))
        grad_v.append(dot(rounded, gs, TN))
    low = jnp.concatenate([grad_k[0] + grad_k[1][:half], grad_v[0] + grad_v[1][:half]], axis=1)
    high = jnp.concatenate([grad_k[1][half:], grad_v[1][half:]], axis=1)
    both = jnp.concatenate([low, high], axis=0).astype(BF16)
    total[...] += dot(x, both, TN)

    @pl.when(step == SEGS - 1)
    def _():
        grad_ref[...] = total[...].astype(BF16)


def local_part(tokens, w_query, w_key, w_value, cot, bias):
    seg = lambda width: pl.BlockSpec((SEG, width), lambda i: (i, 0))
    whole = pl.BlockSpec((D, DH), lambda i: (0, 0), pipeline_mode=pl.Buffered(1))
    return pl.pallas_call(
        local_kernel,
        grid=(SEGS,),
        out_shape=(
            jax.ShapeDtypeStruct((TOK, DH), BF16),
            jax.ShapeDtypeStruct((TOK, DH), F32),
            jax.ShapeDtypeStruct((TOK, DH), F32),
            jax.ShapeDtypeStruct((D, 2 * DH), BF16),
        ),
        in_specs=[seg(D), whole, whole, whole, seg(DH), pl.BlockSpec(memory_space=pltpu.SMEM)],
        out_specs=(seg(DH), seg(DH), seg(DH), pl.BlockSpec((D, 2 * DH), lambda i: (0, 0))),
        scratch_shapes=[pltpu.VMEM((D, 3 * DH), BF16), pltpu.VMEM((D, 2 * DH), F32)],
        compiler_params=pltpu.CompilerParams(
            dimension_semantics=("arbitrary",), vmem_limit_bytes=48 * MIB
        ),
        cost_estimate=pl.CostEstimate(
            flops=14_000_000_000, bytes_accessed=20 * MIB, transcendentals=1_600_000
        ),
        name="local",
    )(tokens, w_query, w_key, w_value, cot, bias)


def memory_kernel(
    counts_ref, slot_ref, bias_ref, tiles_ref, queries_ref, local_ref, ldq_ref, cot_ref, tokens_ref,
    attended_ref, grad_ref, tiles, total, grads, gate_sum, sems,
):
    step = pl.program_id(0)
    per_step = SEG // QB

    @pl.when(step == 0)
    def _():
        total[...] = jnp.zeros_like(total)
        gate_sum[...] = jnp.zeros_like(gate_sum)

        def issue(i, _):
            live = i % TOP < counts_ref[0, i // TOP]

            @pl.when(live)
            def _():
                pltpu.make_async_copy(tiles_ref.at[slot_ref[0, i]], tiles.at[i], sems.at[i]).start()

            @pl.when(jnp.logical_not(live))
            def _():
                tiles[i] = jnp.zeros((2, TILE, DH), BF16)

            return 0

        lax.fori_loop(0, ENTRIES, issue, 0)

    def arrive(i, _):
        entry = step * (per_step * TOP) + i

        @pl.when(entry % TOP < counts_ref[0, entry // TOP])
        def _():
            pltpu.make_async_copy(tiles_ref.at[0], tiles.at[entry], sems.at[entry]).wait()

        return 0

    lax.fori_loop(0, per_step * TOP, arrive, 0)
    gate = gate_row(bias_ref)
    terms = jnp.zeros((1, DH), F32)
    for part in range(per_step):
        rows = slice(part * QB, (part + 1) * QB)
        block = step * per_step + part
        entries = pl.ds(block * TOP, TOP)
        keys = tiles[entries, 0].reshape(TOP * TILE, DH)
        values = tiles[entries, 1].reshape(TOP * TILE, DH)
        up = cot_ref[rows, :].astype(F32)
        local = local_ref[rows, :]
        scores = dot(queries_ref[rows, :], keys, NT) * SCALING
        live = iota((QB, TOP * TILE), 1) < counts_ref[0, block] * TILE
        scores = jnp.where(live, scores, -jnp.inf)
        raised = jnp.exp(scores - jnp.max(scores, axis=1, keepdims=True))
        probs = raised * (1.0 / jnp.sum(raised, axis=1, keepdims=True))
        out = dot(probs.astype(BF16), values)
        back = dot((gate * up).astype(BF16), values, NT)
        dscore = probs * (back - jnp.sum(back * probs, axis=1, keepdims=True)) * SCALING
        dq = dot(dscore.astype(BF16), keys)
        attended_ref[rows, :] = (gate * out + (1.0 - gate) * local).astype(BF16)
        terms += jnp.sum(up * (out - local), axis=0, keepdims=True)
        grads[rows, :] = (dq + ldq_ref[rows, :]).astype(BF16)
    gate_sum[...] += terms
    total[...] += dot(tokens_ref[...], grads[...], TN)

    @pl.when(step == SEGS - 1)
    def _():
        grad_ref[:, :ROWS_OUT, :] = total[...].astype(BF16).reshape(8, ROWS_OUT, DH)
        term = gate_sum[...]
        high = term.astype(BF16)
        rest = term - high.astype(F32)
        mid = rest.astype(BF16)
        low = (rest - mid.astype(F32)).astype(BF16)
        at = iota((GATE_ROWS, DH), 0)
        spread = lambda row: jnp.broadcast_to(row.astype(F32), (GATE_ROWS, DH))
        extra = jnp.where(at == 0, spread(high), jnp.where(at == 1, spread(mid), spread(low)))
        extra = jnp.where(at < 3, extra, 0.0).astype(BF16)
        for owner in range(8):
            grad_ref[owner, ROWS_OUT:, :] = extra


def memory_part(counts, slots, bias, tiles, queries, local, ldq, cot, tokens):
    seg = lambda width: pl.BlockSpec((SEG, width), lambda i: (i, 0))
    smem = pl.BlockSpec(memory_space=pltpu.SMEM)
    rows = ROWS_OUT + GATE_ROWS
    return pl.pallas_call(
        memory_kernel,
        grid=(SEGS,),
        out_shape=(
            jax.ShapeDtypeStruct((TOK, DH), BF16),
            jax.ShapeDtypeStruct((8, rows, DH), BF16),
        ),
        in_specs=[smem, smem, smem, pl.BlockSpec(memory_space=pl.ANY), seg(DH), seg(DH), seg(DH), seg(DH), seg(D)],
        out_specs=(seg(DH), pl.BlockSpec((8, rows, DH), lambda i: (0, 0, 0))),
        scratch_shapes=[
            pltpu.VMEM((ENTRIES, 2, TILE, DH), BF16),
            pltpu.VMEM((D, DH), F32),
            pltpu.VMEM((SEG, DH), BF16),
            pltpu.VMEM((1, DH), F32),
            pltpu.SemaphoreType.DMA((ENTRIES,)),
        ],
        compiler_params=pltpu.CompilerParams(
            dimension_semantics=("arbitrary",), vmem_limit_bytes=48 * MIB
        ),
        cost_estimate=pl.CostEstimate(
            flops=8_000_000_000, bytes_accessed=24 * MIB, transcendentals=1_600_000
        ),
        name="memory",
    )(counts, slots, bias, tiles, queries, local, ldq, cot, tokens)


def exchange(array, axis):
    return lax.all_to_all(array, axis, split_axis=0, concat_axis=0, tiled=True)


def on_device(
    tokens,
    w_query,
    w_key,
    w_value,
    gate_bias,
    memory_keys,
    memory_values,
    retrieval_ids,
    retrieval_counts,
    cotangent,
):
    hidden = tokens[0]
    cot = cotangent[0]
    counts = retrieval_counts.reshape(1, NQB)
    table, slots = make_requests(retrieval_ids.reshape(NQB, TOP), counts)
    wanted = exchange(table, "mem")
    sent = serve(wanted, memory_keys[0], memory_values[0])
    hidden, sent = lax.optimization_barrier((hidden, sent))
    tiles = exchange(sent, "mem")
    queries, local, ldq, grad_kv = local_part(hidden, w_query, w_key, w_value, cot, gate_bias)
    shares_kv = exchange(grad_kv.reshape(8, ROWS_OUT, 2 * DH), "dp")
    sum_kv = jnp.sum(shares_kv.astype(F32), axis=0)
    attended, grad_q = memory_part(
        counts, slots, gate_bias, tiles, queries, local, ldq, cot, hidden
    )
    shares_q = exchange(grad_q, "dp").astype(F32)
    share_q = jnp.sum(shares_q[:, :ROWS_OUT], axis=0)
    gate = jax.nn.sigmoid(gate_bias)
    gate_total = jnp.sum(shares_q[:, ROWS_OUT : ROWS_OUT + 3]) * gate * (1.0 - gate)
    return (attended[None], share_q, sum_kv[:, :DH], sum_kv[:, DH:], gate_total)


def solution(mesh):
    return jax.shard_map(
        on_device,
        mesh=mesh,
        in_specs=(
            P("dp", None, None),
            P(None, "mem"),
            P(None, "mem"),
            P(None, "mem"),
            P("mem"),
            P("dp", "mem", None),
            P("dp", "mem", None),
            P("dp", "mem", None, None),
            P("dp", "mem", None),
            P("dp", None, "mem"),
        ),
        out_specs=(P("dp", None, "mem"), P("dp", "mem"), P("dp", "mem"), P("dp", "mem"), P("mem")),
        check_vma=False,
    )
```

```python
import functools

import jax
import jax.numpy as jnp
from jax import lax
from jax.experimental import pallas as pl
from jax.experimental.pallas import tpu as pltpu
from jax.sharding import PartitionSpec as P

DH = 128
SEG = 512
QB = 128
TILE = 64
TOP = 8
SEGS = 6
TILES_DEV = 24
TOK = 3072
NQB = 24
CAP = 12
MEMS = 16
SIDE = 4
D = 2048
ENTRIES = NQB * TOP
SCALING = DH ** (-0.5)
ROWS_OUT = D // 8
GATE_ROWS = 16
ZS = 4
LOCAL_SEGS = 2
FIRST = (1, 4, 3, 12)
REST = (5, 15, 7, 13, 2, 8, 6, 14, 9, 11, 10, 0)
F32 = jnp.float32
BF16 = jnp.bfloat16
MIB = 1 << 20

NT = (((1,), (1,)), ((), ()))
TN = (((0,), (0,)), ((), ()))


def dot(a, b, dims=(((1,), (0,)), ((), ()))):
    return lax.dot_general(a, b, dims, preferred_element_type=F32)


def iota(shape, dim):
    return lax.broadcasted_iota(jnp.int32, shape, dim)


def gate_row(bias_ref):
    return 1.0 / (1.0 + jnp.exp(-jnp.full((1, DH), bias_ref[0], F32)))


def request_kernel(ids_ref, counts_ref, table_ref, entry_ref):
    ids = ids_ref[...]
    owner = (ids // TILES_DEV).astype(F32)
    local = (ids % TILES_DEV).astype(F32)
    counts = counts_ref[...].astype(F32)
    by_block = (iota((ENTRIES, NQB), 0) // TOP == iota((ENTRIES, NQB), 1)).astype(F32)
    pick = (iota((ENTRIES, TOP), 0) % TOP == iota((ENTRIES, TOP), 1)).astype(F32)
    owner_col = jnp.sum(dot(by_block, owner) * pick, axis=1, keepdims=True)
    local_col = jnp.sum(dot(by_block, local) * pick, axis=1, keepdims=True)
    count_col = jnp.sum(by_block * counts, axis=1, keepdims=True)
    slot_col = (iota((ENTRIES, 1), 0) % TOP).astype(F32)
    owner_col = jnp.where(slot_col < count_col, owner_col, float(MEMS))
    of_block = (iota((NQB, ENTRIES), 1) // TOP == iota((NQB, ENTRIES), 0)).astype(F32)
    of_slot = (iota((TOP, ENTRIES), 1) % TOP == iota((TOP, ENTRIES), 0)).astype(F32)
    owner_row = jnp.sum(dot(owner, of_slot) * of_block, axis=0, keepdims=True)
    count_row = dot(jnp.broadcast_to(counts, (8, NQB)), of_block)[:1]
    slot_row = (iota((1, ENTRIES), 1) % TOP).astype(F32)
    owner_row = jnp.where(slot_row < count_row, owner_row, float(MEMS))
    earlier = iota((ENTRIES, ENTRIES), 1) < iota((ENTRIES, ENTRIES), 0)
    rank_col = jnp.sum(((owner_col == owner_row) & earlier).astype(F32), axis=1, keepdims=True)
    sends = (owner_row == iota((MEMS, ENTRIES), 0).astype(F32)).astype(F32)
    lane = iota((ENTRIES, 128), 1).astype(F32)
    entry_col = iota((ENTRIES, 1), 0).astype(F32) + 1.0
    table_ref[...] = dot(sends, jnp.where(rank_col == lane, local_col, 0.0)).astype(jnp.int32)
    entry_ref[...] = dot(sends, jnp.where(rank_col == lane, entry_col, 0.0)).astype(jnp.int32)


def make_requests(ids, counts):
    return pl.pallas_call(
        request_kernel,
        out_shape=(
            jax.ShapeDtypeStruct((MEMS, 128), jnp.int32),
            jax.ShapeDtypeStruct((MEMS, 128), jnp.int32),
        ),
        name="request",
    )(ids, counts)


def peer(offset, sign):
    me = lax.axis_index("mem")
    row = lax.rem(me // SIDE + sign * (offset // SIDE) + SIDE, SIDE)
    col = lax.rem(lax.rem(me, SIDE) + sign * (offset % SIDE) + SIDE, SIDE)
    return row * SIDE + col


def serve_kernel(offsets, wanted_ref, keys_ref, values_ref, *refs):
    outs = refs[: len(offsets)]
    held, load_sems, store_sem = refs[len(offsets) :]
    for at, offset in enumerate(offsets):
        dest = peer(offset, 1)
        cols = pl.ds(pl.multiple_of(dest * DH, DH), DH)
        sem = load_sems.at[at]

        def issue(rank, _):
            rows = pl.ds(pl.multiple_of(wanted_ref[dest, rank] * TILE, TILE), TILE)
            pltpu.make_async_copy(keys_ref.at[rows, cols], held.at[at, rank, 0], sem).start()
            pltpu.make_async_copy(values_ref.at[rows, cols], held.at[at, rank, 1], sem).start()
            return 0

        lax.fori_loop(0, CAP, issue, 0, unroll=4)
    for at, out_ref in enumerate(outs):
        pltpu.make_async_copy(out_ref, held.at[at], load_sems.at[at]).wait()
        pltpu.make_async_copy(held.at[at], out_ref, store_sem.at[at]).start()
    for at, out_ref in enumerate(outs):
        pltpu.make_async_copy(held.at[at], out_ref, store_sem.at[at]).wait()


def serve(offsets, wanted, keys, values):
    hbm = pl.BlockSpec(memory_space=pl.ANY)
    n = len(offsets)
    return pl.pallas_call(
        functools.partial(serve_kernel, offsets),
        out_shape=[jax.ShapeDtypeStruct((CAP, 2, TILE, DH), BF16)] * n,
        in_specs=[pl.BlockSpec(memory_space=pltpu.SMEM), hbm, hbm],
        out_specs=[hbm] * n,
        scratch_shapes=[
            pltpu.VMEM((n, CAP, 2, TILE, DH), BF16),
            pltpu.SemaphoreType.DMA((n,)),
            pltpu.SemaphoreType.DMA((n,)),
        ],
        compiler_params=pltpu.CompilerParams(vmem_limit_bytes=48 * MIB),
        cost_estimate=pl.CostEstimate(flops=0, bytes_accessed=n * MIB, transcendentals=0),
        name="serve",
    )(wanted, keys, values)


def local_kernel(
    tokens_ref, wq_ref, wk_ref, wv_ref, cot_ref, bias_ref, *refs
):
    before_ref = refs[0] if len(refs) == 6 else None
    queries_ref, out_ref, dq_ref, total, weights = refs[-5:]
    step = pl.program_id(0)

    @pl.when(step == 0)
    def _():
        weights[:, :DH] = wq_ref[...]
        weights[:, DH : 2 * DH] = wk_ref[...]
        weights[:, 2 * DH :] = wv_ref[...]
        total[...] = jnp.zeros_like(total) if before_ref is None else before_ref[...]

    x = tokens_ref[...]
    qkv = dot(x, weights[...]).astype(BF16)
    q, k, v = qkv[:, :DH], qkv[:, DH : 2 * DH], qkv[:, 2 * DH :]
    queries_ref[...] = q
    gate = gate_row(bias_ref)
    grad = ((1.0 - gate) * cot_ref[...].astype(F32)).astype(BF16)
    half = SEG // 2
    grad_k = []
    grad_v = []
    for part in range(2):
        rows = slice(part * half, (part + 1) * half)
        width = (part + 1) * half
        qs, gs, ks, vs = q[rows], grad[rows], k[:width], v[:width]
        scores = dot(qs, ks, NT) * SCALING
        keep = iota((half, width), 0) + part * half >= iota((half, width), 1)
        scores = jnp.where(keep, scores, -jnp.inf)
        raised = jnp.exp(scores - jnp.max(scores, axis=1, keepdims=True))
        probs = raised * (1.0 / jnp.sum(raised, axis=1, keepdims=True))
        rounded = probs.astype(BF16)
        out_ref[rows, :] = dot(rounded, vs)
        back = dot(gs, vs, NT)
        dscore = probs * (back - jnp.sum(back * probs, axis=1, keepdims=True)) * SCALING
        dround = dscore.astype(BF16)
        dq_ref[rows, :] = dot(dround, ks)
        grad_k.append(dot(dround, qs, TN))
        grad_v.append(dot(rounded, gs, TN))
    low = jnp.concatenate([grad_k[0] + grad_k[1][:half], grad_v[0] + grad_v[1][:half]], axis=1)
    high = jnp.concatenate([grad_k[1][half:], grad_v[1][half:]], axis=1)
    both = jnp.concatenate([low, high], axis=0).astype(BF16)
    total[...] += dot(x, both, TN)


def local_part(start, count, tokens, w_query, w_key, w_value, cot, bias, before):
    seg_in = lambda width: pl.BlockSpec((SEG, width), lambda i: (i + start, 0))
    seg = lambda width: pl.BlockSpec((SEG, width), lambda i: (i, 0))
    once = lambda width: pl.BlockSpec((D, width), lambda i: (0, 0), pipeline_mode=pl.Buffered(1))
    given = () if before is None else (before,)
    return pl.pallas_call(
        local_kernel,
        grid=(count,),
        out_shape=(
            jax.ShapeDtypeStruct((SEG * count, DH), BF16),
            jax.ShapeDtypeStruct((SEG * count, DH), F32),
            jax.ShapeDtypeStruct((SEG * count, DH), F32),
            jax.ShapeDtypeStruct((D, 2 * DH), F32),
        ),
        in_specs=[
            seg_in(D), once(DH), once(DH), once(DH), seg_in(DH), pl.BlockSpec(memory_space=pltpu.SMEM)
        ] + [once(2 * DH)] * len(given),
        out_specs=(seg(DH), seg(DH), seg(DH), once(2 * DH)),
        scratch_shapes=[pltpu.VMEM((D, 3 * DH), BF16)],
        compiler_params=pltpu.CompilerParams(
            dimension_semantics=("arbitrary",), vmem_limit_bytes=32 * MIB
        ),
        cost_estimate=pl.CostEstimate(
            flops=2_400_000_000 * count, bytes_accessed=3 * count * MIB, transcendentals=270_000 * count
        ),
        name="local",
    )(tokens, w_query, w_key, w_value, cot, bias, *given)


CLASSES = ((2, 4), (4, 3), (8, 2))


def attend(block, valid, tiles_n, refs):
    count, gate, tiles, queries_ref, local_ref, ldq_ref, cot_ref, attended_ref, grads = refs
    width = tiles_n * TILE
    rows = pl.ds(pl.multiple_of(block * QB, QB), QB)
    entries = pl.ds(block * TOP, tiles_n)
    keys = tiles[entries, 0].reshape(width, DH)
    values = tiles[entries, 1].reshape(width, DH)
    up = cot_ref[rows, :].astype(F32)
    local = local_ref[rows, :]
    scores = dot(queries_ref[rows, :], keys, NT) * SCALING
    back = dot((gate * up).astype(BF16), values, NT)
    scores = jnp.where(iota((QB, width), 1) < count * TILE, scores, -jnp.inf)
    raised = jnp.exp(scores - jnp.max(scores, axis=1, keepdims=True))
    probs = raised * (1.0 / jnp.sum(raised, axis=1, keepdims=True))
    out = dot(probs.astype(BF16), values)
    dscore = probs * (back - jnp.sum(back * probs, axis=1, keepdims=True)) * SCALING
    dq = dot(dscore.astype(BF16), keys)
    attended_ref[rows, :] = (gate * out + (1.0 - gate) * local).astype(BF16)
    grads[rows, :] = (dq + ldq_ref[rows, :]).astype(BF16)
    term = jnp.sum(up * (out - local), axis=0, keepdims=True)
    return jnp.where(valid, term, 0.0)


def memory_kernel(counts_ref, entry_ref, bias_ref, *refs):
    tile_refs = refs[:MEMS]
    queries_ref, local_ref, ldq_ref, cot_ref, tokens_ref = refs[MEMS : MEMS + 5]
    attended_ref, mine_ref, other_ref = refs[MEMS + 5 : MEMS + 8]
    tiles, tokens, total, grads, gate_sum, lists, sems, token_sems = refs[MEMS + 8 :]

    for offset in range(MEMS):
        source = peer(offset, -1)

        def issue(rank, _):
            entry = entry_ref[source, rank] - 1

            @pl.when(entry >= 0)
            def _():
                pltpu.make_async_copy(
                    tile_refs[offset].at[rank], tiles.at[entry], sems.at[entry]
                ).start()

            return 0

        lax.fori_loop(0, CAP, issue, 0)
    for part in range(SEGS):
        rows = pl.ds(part * SEG, SEG)
        pltpu.make_async_copy(tokens_ref.at[rows], tokens.at[rows], token_sems.at[part]).start()

    def sort(block, sizes):
        count = counts_ref[0, block]
        sizes = list(sizes)
        low = 0
        for at, (tiles_n, _) in enumerate(CLASSES):
            here = (count > low) & (count <= tiles_n)

            @pl.when(here)
            def _(at=at, tiles_n=tiles_n):
                lists[at, sizes[at]] = block

                def clear(slot, _):
                    tiles[block * TOP + slot] = jnp.zeros((2, TILE, DH), BF16)
                    return 0

                lax.fori_loop(count, tiles_n, clear, 0)

            sizes[at] = sizes[at] + here.astype(jnp.int32)
            low = tiles_n
        return tuple(sizes)

    sizes = lax.fori_loop(0, NQB, sort, (jnp.int32(0),) * len(CLASSES))
    gate = gate_row(bias_ref)
    gate_sum[...] = jnp.zeros_like(gate_sum)
    for at, (tiles_n, group) in enumerate(CLASSES):

        def batch(i, _, at=at, tiles_n=tiles_n, group=group):
            members = []
            for k in range(group):
                valid = i * group + k < sizes[at]
                block = lists[at, jnp.minimum(i * group + k, sizes[at] - 1)]
                count = counts_ref[0, block]
                members.append((block, valid, count))

                def arrive(slot, _):
                    entry = block * TOP + slot
                    pltpu.make_async_copy(
                        tile_refs[0].at[0], tiles.at[entry], sems.at[entry]
                    ).wait()
                    return 0

                lax.fori_loop(0, jnp.where(valid, count, 0), arrive, 0)
            terms = jnp.zeros((1, DH), F32)
            for block, valid, count in members:
                terms += attend(
                    block, valid, tiles_n,
                    (count, gate, tiles, queries_ref, local_ref, ldq_ref, cot_ref, attended_ref, grads),
                )
            gate_sum[...] += terms
            return 0

        lax.fori_loop(0, pl.cdiv(sizes[at], group), batch, 0)
    for part in range(SEGS):
        rows = pl.ds(part * SEG, SEG)
        pltpu.make_async_copy(tokens_ref.at[rows], tokens.at[rows], token_sems.at[part]).wait()
        term = dot(grads[rows, :], tokens[rows, :], TN)
        if part == 0:
            total[...] = term
        else:
            total[...] += term
    turned = total[...].T
    core = lax.rem(lax.axis_index("dp"), 2)
    extra = split_gate(gate_sum[...])
    for z in range(ZS):
        low = turned[2 * z * ROWS_OUT : (2 * z + 1) * ROWS_OUT]
        high = turned[(2 * z + 1) * ROWS_OUT : (2 * z + 2) * ROWS_OUT]
        mine_ref[z, :ROWS_OUT, :] = jnp.where(core == 0, low, high)
        mine_ref[z, ROWS_OUT:, :] = extra.astype(F32)
        other_ref[z, :ROWS_OUT, :] = jnp.where(core == 0, high, low).astype(BF16)
        other_ref[z, ROWS_OUT:, :] = extra


def split_gate(term):
    high = term.astype(BF16)
    rest = term - high.astype(F32)
    mid = rest.astype(BF16)
    low = (rest - mid.astype(F32)).astype(BF16)
    at = iota((GATE_ROWS, DH), 0)
    spread = lambda row: jnp.broadcast_to(row.astype(F32), (GATE_ROWS, DH))
    extra = jnp.where(at == 0, spread(high), jnp.where(at == 1, spread(mid), spread(low)))
    return jnp.where(at < 3, extra, 0.0).astype(BF16)


def memory_part(counts, entries, bias, tiles, queries, local, ldq, cot, tokens):
    smem = pl.BlockSpec(memory_space=pltpu.SMEM)
    vmem = pl.BlockSpec(memory_space=pltpu.VMEM)
    hbm = pl.BlockSpec(memory_space=pl.ANY)
    rows = ROWS_OUT + GATE_ROWS
    return pl.pallas_call(
        memory_kernel,
        out_shape=(
            jax.ShapeDtypeStruct((TOK, DH), BF16),
            jax.ShapeDtypeStruct((ZS, rows, DH), F32),
            jax.ShapeDtypeStruct((ZS, rows, DH), BF16),
        ),
        in_specs=[smem] * 3 + [hbm] * MEMS + [vmem] * 4 + [hbm],
        out_specs=(vmem, vmem, vmem),
        scratch_shapes=[
            pltpu.VMEM((ENTRIES, 2, TILE, DH), BF16),
            pltpu.VMEM((TOK, D), BF16),
            pltpu.VMEM((DH, D), F32),
            pltpu.VMEM((TOK, DH), BF16),
            pltpu.VMEM((1, DH), F32),
            pltpu.SMEM((len(CLASSES), 32), jnp.int32),
            pltpu.SemaphoreType.DMA((ENTRIES,)),
            pltpu.SemaphoreType.DMA((SEGS,)),
        ],
        compiler_params=pltpu.CompilerParams(vmem_limit_bytes=40 * MIB),
        cost_estimate=pl.CostEstimate(
            flops=8_000_000_000, bytes_accessed=24 * MIB, transcendentals=1_600_000
        ),
        name="memory",
    )(counts, entries, bias, *tiles, queries, local, ldq, cot, tokens)


def pair_kernel(mine_ref, got_ref, *outs):
    z = lax.axis_index("dp") // 2
    for step in range(ZS):
        at = lax.rem(z + step, ZS)
        both = mine_ref[at] + got_ref[at].astype(F32)
        gate = jnp.sum(both[ROWS_OUT : ROWS_OUT + 3], axis=0, keepdims=True)
        extra = split_gate(gate)
        outs[step][:ROWS_OUT, :] = both[:ROWS_OUT].astype(outs[step].dtype)
        outs[step][ROWS_OUT:, :] = extra.astype(outs[step].dtype)


def pair_sum(mine, got):
    rows = mine.shape[1:]
    return pl.pallas_call(
        pair_kernel,
        out_shape=[jax.ShapeDtypeStruct(rows, F32)] + [jax.ShapeDtypeStruct(rows, BF16)] * (ZS - 1),
        name="pair",
    )(mine, got)


def last_kernel(bias_ref, own_ref, one_ref, two_ref, three_ref, share_ref, gate_ref):
    sums = own_ref[...] + one_ref[...].astype(F32) + two_ref[...].astype(F32) + three_ref[...].astype(F32)
    share_ref[...] = sums[:ROWS_OUT]
    gate = gate_row(bias_ref)
    term = jnp.sum(sums[ROWS_OUT : ROWS_OUT + 3], axis=0, keepdims=True)
    whole = jnp.sum(term, axis=1, keepdims=True)
    gate_ref[...] = jnp.broadcast_to(whole, (1, DH)) * gate * (1.0 - gate)


def last_sum(bias, parts):
    vmem = pl.BlockSpec(memory_space=pltpu.VMEM)
    return pl.pallas_call(
        last_kernel,
        out_shape=(jax.ShapeDtypeStruct((ROWS_OUT, DH), F32), jax.ShapeDtypeStruct((1, DH), F32)),
        in_specs=[pl.BlockSpec(memory_space=pltpu.SMEM)] + [vmem] * ZS,
        out_specs=(vmem, vmem),
        name="last",
    )(bias, *parts)


def swap_cores(array):
    return lax.ppermute(array, "dp", [(i, i ^ 1) for i in range(2 * ZS)])


def along_z(array, step):
    return lax.ppermute(array, "dp", [(i, (i + 2 * step) % (2 * ZS)) for i in range(2 * ZS)])


def along_mem(array, offset):
    pairs = []
    for i in range(MEMS):
        row = (i // SIDE + offset // SIDE) % SIDE
        col = (i % SIDE + offset % SIDE) % SIDE
        pairs.append((i, row * SIDE + col))
    return lax.ppermute(array, "mem", pairs)


def exchange(array, axis):
    return lax.all_to_all(array, axis, split_axis=0, concat_axis=0, tiled=True)


def on_device(
    tokens,
    w_query,
    w_key,
    w_value,
    gate_bias,
    memory_keys,
    memory_values,
    retrieval_ids,
    retrieval_counts,
    cotangent,
):
    hidden = tokens[0]
    cot = cotangent[0]
    counts = retrieval_counts.reshape(1, NQB)
    table, entries = make_requests(retrieval_ids.reshape(NQB, TOP), counts)
    wanted = exchange(table, "mem")
    keys, values = memory_keys[0], memory_values[0]
    tiles = [None] * MEMS
    for offset, sent in zip(FIRST, serve(FIRST, wanted, keys, values)):
        tiles[offset] = along_mem(sent, offset)
    for offset, sent in zip(REST, serve(REST, wanted, keys, values)):
        tiles[offset] = along_mem(sent, offset) if offset else sent
    hidden, own = lax.optimization_barrier((hidden, tiles[0]))
    tiles[0] = own
    grad_kv = None
    pieces = []
    for start in range(0, SEGS, LOCAL_SEGS):
        *piece, grad_kv = local_part(
            start, LOCAL_SEGS, hidden, w_query, w_key, w_value, cot, gate_bias, grad_kv
        )
        pieces.append(piece)
    queries, local, ldq = (jnp.concatenate(parts, axis=0) for parts in zip(*pieces))
    shares_kv = exchange(grad_kv.astype(BF16).reshape(8, ROWS_OUT, 2 * DH), "dp")
    sum_kv = jnp.sum(shares_kv.astype(F32), axis=0)
    attended, mine, other = memory_part(
        counts, entries, gate_bias, tiles, queries, local, ldq, cot, hidden
    )
    own, *others = pair_sum(mine, swap_cores(other))
    parts = [own] + [along_z(part, step + 1) for step, part in enumerate(others)]
    share_q, gate_total = last_sum(gate_bias, parts)
    return (attended[None], share_q, sum_kv[:, :DH], sum_kv[:, DH:], gate_total[0, :1])


def solution(mesh):
    return jax.shard_map(
        on_device,
        mesh=mesh,
        in_specs=(
            P("dp", None, None),
            P(None, "mem"),
            P(None, "mem"),
            P(None, "mem"),
            P("mem"),
            P("dp", "mem", None),
            P("dp", "mem", None),
            P("dp", "mem", None, None),
            P("dp", "mem", None),
            P("dp", None, "mem"),
        ),
        out_specs=(P("dp", None, "mem"), P("dp", "mem"), P("dp", "mem"), P("dp", "mem"), P("mem")),
        check_vma=False,
    )
```

```python
import functools

import jax
import jax.numpy as jnp
from jax import lax
from jax.experimental import pallas as pl
from jax.experimental.pallas import tpu as pltpu
from jax.sharding import PartitionSpec as P

DH = 128
SEG = 512
QB = 128
TILE = 64
TOP = 8
SEGS = 6
TILES_DEV = 24
TOK = 3072
NQB = 24
CAP = 12
MEMS = 16
D = 2048
ENTRIES = NQB * TOP
SCALING = DH ** (-0.5)
ROWS_OUT = D // 8
GATE_ROWS = 16
ZS = 4
F32 = jnp.float32
BF16 = jnp.bfloat16
MIB = 1 << 20

NT = (((1,), (1,)), ((), ()))
TN = (((0,), (0,)), ((), ()))


def dot(a, b, dims=(((1,), (0,)), ((), ()))):
    return lax.dot_general(a, b, dims, preferred_element_type=F32)


def iota(shape, dim):
    return lax.broadcasted_iota(jnp.int32, shape, dim)


def gate_row(bias_ref):
    return 1.0 / (1.0 + jnp.exp(-jnp.full((1, DH), bias_ref[0], F32)))


def request_kernel(ids_ref, counts_ref, table_ref, slot_ref):
    ids = ids_ref[...]
    owner = (ids // TILES_DEV).astype(F32)
    local = (ids % TILES_DEV).astype(F32)
    counts = counts_ref[...].astype(F32)
    by_block = (iota((ENTRIES, NQB), 0) // TOP == iota((ENTRIES, NQB), 1)).astype(F32)
    pick = (iota((ENTRIES, TOP), 0) % TOP == iota((ENTRIES, TOP), 1)).astype(F32)
    owner_col = jnp.sum(dot(by_block, owner) * pick, axis=1, keepdims=True)
    local_col = jnp.sum(dot(by_block, local) * pick, axis=1, keepdims=True)
    count_col = jnp.sum(by_block * counts, axis=1, keepdims=True)
    slot_col = (iota((ENTRIES, 1), 0) % TOP).astype(F32)
    owner_col = jnp.where(slot_col < count_col, owner_col, float(MEMS))
    of_block = (iota((NQB, ENTRIES), 1) // TOP == iota((NQB, ENTRIES), 0)).astype(F32)
    of_slot = (iota((TOP, ENTRIES), 1) % TOP == iota((TOP, ENTRIES), 0)).astype(F32)
    owner_row = jnp.sum(dot(owner, of_slot) * of_block, axis=0, keepdims=True)
    count_row = dot(jnp.broadcast_to(counts, (8, NQB)), of_block)[:1]
    slot_row = (iota((1, ENTRIES), 1) % TOP).astype(F32)
    owner_row = jnp.where(slot_row < count_row, owner_row, float(MEMS))
    same = owner_col == owner_row
    first = iota((ENTRIES, ENTRIES), 0)
    second = iota((ENTRIES, ENTRIES), 1)
    rank_col = jnp.sum((same & (second < first)).astype(F32), axis=1, keepdims=True)
    rank_row = jnp.sum((same & (first < second)).astype(F32), axis=0, keepdims=True)
    sends = (owner_row == iota((MEMS, ENTRIES), 0).astype(F32)).astype(F32)
    place = jnp.where(rank_col == iota((ENTRIES, 128), 1).astype(F32), local_col, 0.0)
    table_ref[...] = dot(sends, place).astype(jnp.int32)
    slot_ref[...] = jnp.clip(owner_row * CAP + rank_row, 0.0, float(MEMS * CAP - 1)).astype(jnp.int32)


def make_requests(ids, counts):
    return pl.pallas_call(
        request_kernel,
        out_shape=(
            jax.ShapeDtypeStruct((MEMS, 128), jnp.int32),
            jax.ShapeDtypeStruct((1, ENTRIES), jnp.int32),
        ),
        name="request",
    )(ids, counts)


def serve_kernel(wanted_ref, keys_ref, values_ref, out_ref, held, load_sems, store_sem):
    def issue(i, _):
        dest = i // CAP
        rank = i % CAP
        rows = pl.ds(pl.multiple_of(wanted_ref[dest, rank] * TILE, TILE), TILE)
        cols = pl.ds(pl.multiple_of(dest * DH, DH), DH)
        sem = load_sems.at[dest]
        pltpu.make_async_copy(keys_ref.at[rows, cols], held.at[i, 0], sem).start()
        pltpu.make_async_copy(values_ref.at[rows, cols], held.at[i, 1], sem).start()
        return 0

    lax.fori_loop(0, MEMS * CAP, issue, 0, unroll=4)
    for dest in range(MEMS):
        mine = pl.ds(dest * CAP, CAP)
        pltpu.make_async_copy(out_ref.at[mine], held.at[mine], load_sems.at[dest]).wait()
        pltpu.make_async_copy(held.at[mine], out_ref.at[mine], store_sem).start()
    pltpu.make_async_copy(held, out_ref, store_sem).wait()


def serve(wanted, keys, values):
    hbm = pl.BlockSpec(memory_space=pl.ANY)
    return pl.pallas_call(
        serve_kernel,
        out_shape=jax.ShapeDtypeStruct((MEMS * CAP, 2, TILE, DH), BF16),
        in_specs=[pl.BlockSpec(memory_space=pltpu.SMEM), hbm, hbm],
        out_specs=hbm,
        scratch_shapes=[
            pltpu.VMEM((MEMS * CAP, 2, TILE, DH), BF16),
            pltpu.SemaphoreType.DMA((MEMS,)),
            pltpu.SemaphoreType.DMA(()),
        ],
        compiler_params=pltpu.CompilerParams(vmem_limit_bytes=48 * MIB),
        cost_estimate=pl.CostEstimate(flops=0, bytes_accessed=12 * MIB, transcendentals=0),
        name="serve",
    )(wanted, keys, values)


def local_kernel(
    tokens_ref, wq_ref, wk_ref, wv_ref, cot_ref, bias_ref,
    queries_ref, out_ref, dq_ref, mine_ref, other_ref, weights, total,
):
    step = pl.program_id(0)

    @pl.when(step == 0)
    def _():
        weights[:, :DH] = wq_ref[...]
        weights[:, DH : 2 * DH] = wk_ref[...]
        weights[:, 2 * DH :] = wv_ref[...]
        total[...] = jnp.zeros_like(total)

    x = tokens_ref[...]
    qkv = dot(x, weights[...]).astype(BF16)
    q, k, v = qkv[:, :DH], qkv[:, DH : 2 * DH], qkv[:, 2 * DH :]
    queries_ref[...] = q
    gate = gate_row(bias_ref)
    grad = ((1.0 - gate) * cot_ref[...].astype(F32)).astype(BF16)
    half = SEG // 2
    grad_k = []
    grad_v = []
    for part in range(2):
        rows = slice(part * half, (part + 1) * half)
        width = (part + 1) * half
        qs, gs, ks, vs = q[rows], grad[rows], k[:width], v[:width]
        scores = dot(qs, ks, NT) * SCALING
        keep = iota((half, width), 0) + part * half >= iota((half, width), 1)
        scores = jnp.where(keep, scores, -jnp.inf)
        raised = jnp.exp(scores - jnp.max(scores, axis=1, keepdims=True))
        probs = raised * (1.0 / jnp.sum(raised, axis=1, keepdims=True))
        rounded = probs.astype(BF16)
        out_ref[rows, :] = dot(rounded, vs)
        back = dot(gs, vs, NT)
        dscore = probs * (back - jnp.sum(back * probs, axis=1, keepdims=True)) * SCALING
        dround = dscore.astype(BF16)
        dq_ref[rows, :] = dot(dround, ks)
        grad_k.append(dot(dround, qs, TN))
        grad_v.append(dot(rounded, gs, TN))
    low = jnp.concatenate([grad_k[0] + grad_k[1][:half], grad_v[0] + grad_v[1][:half]], axis=1)
    high = jnp.concatenate([grad_k[1][half:], grad_v[1][half:]], axis=1)
    both = jnp.concatenate([low, high], axis=0).astype(BF16)
    total[...] += dot(x, both, TN)

    @pl.when(step == SEGS - 1)
    def _():
        me = lax.axis_index("dp")
        core = lax.rem(me, 2)
        for z in range(ZS):
            owner = lax.rem(me // 2 + z, ZS) * 2
            for part_ref, side in ((mine_ref, core), (other_ref, 1 - core)):
                at = pl.ds(pl.multiple_of((owner + side) * ROWS_OUT, ROWS_OUT), ROWS_OUT)
                part_ref[z] = total[at, :].astype(part_ref.dtype)


def local_part(tokens, w_query, w_key, w_value, cot, bias):
    seg = lambda width: pl.BlockSpec((SEG, width), lambda i: (i, 0))
    whole = pl.BlockSpec((D, DH), lambda i: (0, 0), pipeline_mode=pl.Buffered(1))
    fixed = pl.BlockSpec((ZS, ROWS_OUT, 2 * DH), lambda i: (0, 0, 0))
    return pl.pallas_call(
        local_kernel,
        grid=(SEGS,),
        out_shape=(
            jax.ShapeDtypeStruct((TOK, DH), BF16),
            jax.ShapeDtypeStruct((TOK, DH), F32),
            jax.ShapeDtypeStruct((TOK, DH), F32),
            jax.ShapeDtypeStruct((ZS, ROWS_OUT, 2 * DH), F32),
            jax.ShapeDtypeStruct((ZS, ROWS_OUT, 2 * DH), BF16),
        ),
        in_specs=[seg(D), whole, whole, whole, seg(DH), pl.BlockSpec(memory_space=pltpu.SMEM)],
        out_specs=(seg(DH), seg(DH), seg(DH), fixed, fixed),
        scratch_shapes=[pltpu.VMEM((D, 3 * DH), BF16), pltpu.VMEM((D, 2 * DH), F32)],
        compiler_params=pltpu.CompilerParams(
            dimension_semantics=("arbitrary",), vmem_limit_bytes=48 * MIB
        ),
        cost_estimate=pl.CostEstimate(
            flops=14_000_000_000, bytes_accessed=20 * MIB, transcendentals=1_600_000
        ),
        name="local",
    )(tokens, w_query, w_key, w_value, cot, bias)


CLASSES = ((2, 6), (4, 3), (8, 3))


def attend_all(members, tiles_n, refs):
    gate, tiles, queries_ref, local_ref, ldq_ref, cot_ref, attended_ref, grads = refs
    width = tiles_n * TILE
    at = [pl.ds(pl.multiple_of(block * QB, QB), QB) for block, _, _ in members]
    entries = [pl.ds(block * TOP, tiles_n) for block, _, _ in members]
    keys = [tiles[e, 0].reshape(width, DH) for e in entries]
    values = [tiles[e, 1].reshape(width, DH) for e in entries]
    up = [cot_ref[rows, :].astype(F32) for rows in at]
    queries = [queries_ref[rows, :] for rows in at]
    scores = [dot(k, q, NT) for k, q in zip(keys, queries)]
    back = [dot(v, (gate * u).astype(BF16), NT) for v, u in zip(values, up)]
    probs = []
    for s, (_, _, count) in zip(scores, members):
        s = jnp.where(iota((width, QB), 0) < count * TILE, s * SCALING, -jnp.inf)
        raised = jnp.exp(s - jnp.max(s, axis=0, keepdims=True))
        probs.append(raised * (1.0 / jnp.sum(raised, axis=0, keepdims=True)))
    out = [dot(p.astype(BF16), v, TN) for p, v in zip(probs, values)]
    dscore = [
        p * (b - jnp.sum(b * p, axis=0, keepdims=True)) * SCALING for p, b in zip(probs, back)
    ]
    dq = [dot(d.astype(BF16), k, TN) for d, k in zip(dscore, keys)]
    local = [local_ref[rows, :] for rows in at]
    ldq = [ldq_ref[rows, :] for rows in at]
    terms = jnp.zeros((1, DH), F32)
    for u, o, lo, (_, valid, _) in zip(up, out, local, members):
        terms += jnp.where(valid, jnp.sum(u * (o - lo), axis=0, keepdims=True), 0.0)
    for rows, o, lo, d, ld in zip(at, out, local, dq, ldq):
        attended_ref[rows, :] = (gate * o + (1.0 - gate) * lo).astype(BF16)
        grads[rows, :] = (d + ld).astype(BF16)
    return terms


def memory_kernel(
    counts_ref, slot_ref, bias_ref, tiles_ref, queries_ref, local_ref, ldq_ref, cot_ref, tokens_ref,
    attended_ref, mine_ref, other_ref, tiles, tokens, total, grads, gate_sum, lists, sems, token_sems,
):
    def sort(block, sizes):
        count = counts_ref[0, block]

        def fetch(slot, _):
            entry = block * TOP + slot
            pltpu.make_async_copy(tiles_ref.at[slot_ref[0, entry]], tiles.at[entry], sems.at[entry]).start()
            return 0

        lax.fori_loop(0, count, fetch, 0)
        sizes = list(sizes)
        low = 0
        for at, (tiles_n, _) in enumerate(CLASSES):
            here = (count > low) & (count <= tiles_n)

            @pl.when(here)
            def _(at=at, tiles_n=tiles_n):
                lists[at, sizes[at]] = block

                def clear(slot, _):
                    tiles[block * TOP + slot] = jnp.zeros((2, TILE, DH), BF16)
                    return 0

                lax.fori_loop(count, tiles_n, clear, 0)

            sizes[at] = sizes[at] + here.astype(jnp.int32)
            low = tiles_n
        return tuple(sizes)

    sizes = lax.fori_loop(0, NQB, sort, (jnp.int32(0),) * len(CLASSES))
    for part in range(SEGS):
        rows = pl.ds(part * SEG, SEG)
        pltpu.make_async_copy(tokens_ref.at[rows], tokens.at[rows], token_sems.at[part]).start()
    gate = gate_row(bias_ref)
    gate_sum[...] = jnp.zeros_like(gate_sum)
    for at, (tiles_n, group) in enumerate(CLASSES):

        def batch(i, _, at=at, tiles_n=tiles_n, group=group):
            members = []
            for k in range(group):
                valid = i * group + k < sizes[at]
                block = lists[at, jnp.minimum(i * group + k, sizes[at] - 1)]
                count = counts_ref[0, block]
                members.append((block, valid, count))

                def arrive(slot, _):
                    entry = block * TOP + slot
                    pltpu.make_async_copy(
                        tiles_ref.at[0], tiles.at[entry], sems.at[entry]
                    ).wait()
                    return 0

                lax.fori_loop(0, jnp.where(valid, count, 0), arrive, 0)
            terms = attend_all(
                members, tiles_n,
                (gate, tiles, queries_ref, local_ref, ldq_ref, cot_ref, attended_ref, grads),
            )
            gate_sum[...] += terms
            return 0

        lax.fori_loop(0, pl.cdiv(sizes[at], group), batch, 0)
    for part in range(SEGS):
        rows = pl.ds(part * SEG, SEG)
        pltpu.make_async_copy(tokens_ref.at[rows], tokens.at[rows], token_sems.at[part]).wait()
        term = dot(grads[rows, :], tokens[rows, :], TN)
        if part == 0:
            total[...] = term
        else:
            total[...] += term
    me = lax.axis_index("dp")
    core = lax.rem(me, 2)
    extra = split_gate(gate_sum[...])
    for step in range(ZS):
        owner = lax.rem(me // 2 + step, ZS) * 2
        for out_ref, side in ((mine_ref, core), (other_ref, 1 - core)):
            cols = pl.ds(pl.multiple_of((owner + side) * ROWS_OUT, ROWS_OUT), ROWS_OUT)
            out_ref[step, :ROWS_OUT, :] = total[:, cols].T.astype(out_ref.dtype)
        mine_ref[step, ROWS_OUT:, :] = extra[0]
        other_ref[step, ROWS_OUT:, :] = extra[1].astype(BF16)


def split_gate(term):
    high = term.astype(BF16).astype(F32)
    mid = (term - high).astype(BF16).astype(F32)
    low = term - high - mid
    at = iota((GATE_ROWS, DH), 0)
    spread = lambda row: jnp.broadcast_to(row, (GATE_ROWS, DH))
    parts = []
    for first in (0, 3):
        row = jnp.where(at == first, spread(high), jnp.where(at == first + 1, spread(mid), spread(low)))
        parts.append(jnp.where((at >= first) & (at < first + 3), row, 0.0))
    return parts


def memory_part(counts, slots, bias, tiles, queries, local, ldq, cot, tokens):
    smem = pl.BlockSpec(memory_space=pltpu.SMEM)
    vmem = pl.BlockSpec(memory_space=pltpu.VMEM)
    hbm = pl.BlockSpec(memory_space=pl.ANY)
    rows = ROWS_OUT + GATE_ROWS
    return pl.pallas_call(
        memory_kernel,
        out_shape=(
            jax.ShapeDtypeStruct((TOK, DH), BF16),
            jax.ShapeDtypeStruct((ZS, rows, DH), F32),
            jax.ShapeDtypeStruct((ZS, rows, DH), BF16),
        ),
        in_specs=[smem] * 3 + [hbm] + [vmem] * 4 + [hbm],
        out_specs=(vmem, vmem, vmem),
        scratch_shapes=[
            pltpu.VMEM((ENTRIES, 2, TILE, DH), BF16),
            pltpu.VMEM((TOK, D), BF16),
            pltpu.VMEM((DH, D), F32),
            pltpu.VMEM((TOK, DH), BF16),
            pltpu.VMEM((1, DH), F32),
            pltpu.SMEM((len(CLASSES), 32), jnp.int32),
            pltpu.SemaphoreType.DMA((ENTRIES,)),
            pltpu.SemaphoreType.DMA((SEGS,)),
        ],
        compiler_params=pltpu.CompilerParams(vmem_limit_bytes=48 * MIB),
        cost_estimate=pl.CostEstimate(
            flops=8_000_000_000, bytes_accessed=24 * MIB, transcendentals=1_600_000
        ),
        name="memory",
    )(counts, slots, bias, tiles, queries, local, ldq, cot, tokens)


def swap_cores(array):
    return lax.ppermute(array, "dp", [(i, i ^ 1) for i in range(2 * ZS)])


def along_z(array, step):
    return lax.ppermute(array, "dp", [(i, (i + 2 * step) % (2 * ZS)) for i in range(2 * ZS)])


def reduce_docs(mine, other):
    got = swap_cores(other)
    total = mine[0] + got[0].astype(F32)
    for step in range(1, ZS):
        both = (mine[step] + got[step].astype(F32)).astype(BF16)
        total = total + along_z(both, step).astype(F32)
    return total


def exchange(array, axis):
    return lax.all_to_all(array, axis, split_axis=0, concat_axis=0, tiled=True)


def on_device(
    tokens,
    w_query,
    w_key,
    w_value,
    gate_bias,
    memory_keys,
    memory_values,
    retrieval_ids,
    retrieval_counts,
    cotangent,
):
    hidden = tokens[0]
    cot = cotangent[0]
    counts = retrieval_counts.reshape(1, NQB)
    table, slots = make_requests(retrieval_ids.reshape(NQB, TOP), counts)
    wanted = exchange(table, "mem")
    sent = serve(wanted, memory_keys[0], memory_values[0])
    hidden, sent = lax.optimization_barrier((hidden, sent))
    tiles = exchange(sent, "mem")
    queries, local, ldq, mine, other = local_part(hidden, w_query, w_key, w_value, cot, gate_bias)
    sum_kv = reduce_docs(mine, other)
    share_k, share_v = sum_kv[:, :DH], sum_kv[:, DH:]
    counts, share_k, share_v = lax.optimization_barrier((counts, share_k, share_v))
    attended, mine, other = memory_part(
        counts, slots, gate_bias, tiles, queries, local, ldq, cot, hidden
    )
    total = reduce_docs(mine, other)
    gate = jax.nn.sigmoid(gate_bias)
    gate_total = jnp.sum(total[ROWS_OUT : ROWS_OUT + 6]) * gate * (1.0 - gate)
    return (attended[None], total[:ROWS_OUT], share_k, share_v, gate_total)


def solution(mesh):
    return jax.shard_map(
        on_device,
        mesh=mesh,
        in_specs=(
            P("dp", None, None),
            P(None, "mem"),
            P(None, "mem"),
            P(None, "mem"),
            P("mem"),
            P("dp", "mem", None),
            P("dp", "mem", None),
            P("dp", "mem", None, None),
            P("dp", "mem", None),
            P("dp", None, "mem"),
        ),
        out_specs=(P("dp", None, "mem"), P("dp", "mem"), P("dp", "mem"), P("dp", "mem"), P("mem")),
        check_vma=False,
    )
```

```python
import functools

import jax
import jax.numpy as jnp
from jax import lax
from jax.experimental import pallas as pl
from jax.experimental.pallas import tpu as pltpu
from jax.sharding import PartitionSpec as P

DH = 128
SEG = 512
QB = 128
TILE = 64
TOP = 8
SEGS = 6
TILES_DEV = 24
TOK = 3072
NQB = 24
CAP = 12
MEMS = 16
D = 2048
ENTRIES = NQB * TOP
SCALING = DH ** (-0.5)
ROWS_OUT = D // 8
GATE_ROWS = 16
ZS = 4
F32 = jnp.float32
BF16 = jnp.bfloat16
MIB = 1 << 20

NT = (((1,), (1,)), ((), ()))
TN = (((0,), (0,)), ((), ()))


def dot(a, b, dims=(((1,), (0,)), ((), ()))):
    return lax.dot_general(a, b, dims, preferred_element_type=F32)


def iota(shape, dim):
    return lax.broadcasted_iota(jnp.int32, shape, dim)


def gate_row(bias_ref):
    return 1.0 / (1.0 + jnp.exp(-jnp.full((1, DH), bias_ref[0], F32)))


def request_kernel(ids_ref, counts_ref, table_ref, slot_ref):
    ids = ids_ref[...]
    owner = (ids // TILES_DEV).astype(F32)
    local = (ids % TILES_DEV).astype(F32)
    counts = counts_ref[...].astype(F32)
    by_block = (iota((ENTRIES, NQB), 0) // TOP == iota((ENTRIES, NQB), 1)).astype(F32)
    pick = (iota((ENTRIES, TOP), 0) % TOP == iota((ENTRIES, TOP), 1)).astype(F32)
    owner_col = jnp.sum(dot(by_block, owner, NT) * pick, axis=1, keepdims=True)
    local_col = jnp.sum(dot(by_block, local, NT) * pick, axis=1, keepdims=True)
    count_col = jnp.sum(by_block * counts, axis=1, keepdims=True)
    slot_col = (iota((ENTRIES, 1), 0) % TOP).astype(F32)
    owner_col = jnp.where(slot_col < count_col, owner_col, float(MEMS))
    of_block = (iota((NQB, ENTRIES), 1) // TOP == iota((NQB, ENTRIES), 0)).astype(F32)
    of_slot = (iota((TOP, ENTRIES), 1) % TOP == iota((TOP, ENTRIES), 0)).astype(F32)
    owner_row = jnp.sum(dot(owner, of_slot, TN) * of_block, axis=0, keepdims=True)
    count_row = dot(jnp.broadcast_to(counts, (8, NQB)), of_block)[:1]
    slot_row = (iota((1, ENTRIES), 1) % TOP).astype(F32)
    owner_row = jnp.where(slot_row < count_row, owner_row, float(MEMS))
    same = owner_col == owner_row
    first = iota((ENTRIES, ENTRIES), 0)
    second = iota((ENTRIES, ENTRIES), 1)
    rank_col = jnp.sum((same & (second < first)).astype(F32), axis=1, keepdims=True)
    rank_row = jnp.sum((same & (first < second)).astype(F32), axis=0, keepdims=True)
    sends = (owner_row == iota((MEMS, ENTRIES), 0).astype(F32)).astype(F32)
    place = jnp.where(rank_col == iota((ENTRIES, 128), 1).astype(F32), local_col, 0.0)
    table_ref[...] = dot(sends, place).astype(jnp.int32)
    slot_ref[...] = jnp.clip(owner_row * CAP + rank_row, 0.0, float(MEMS * CAP - 1)).astype(jnp.int32)


def make_requests(ids, counts):
    return pl.pallas_call(
        request_kernel,
        out_shape=(
            jax.ShapeDtypeStruct((MEMS, 128), jnp.int32),
            jax.ShapeDtypeStruct((1, ENTRIES), jnp.int32),
        ),
        name="request",
    )(ids, counts)


def serve_kernel(wanted_ref, keys_ref, values_ref, out_ref, held, load_sems, store_sem):
    def issue(i, _):
        dest = i // CAP
        rank = i % CAP
        rows = pl.ds(pl.multiple_of(wanted_ref[dest, rank] * TILE, TILE), TILE)
        cols = pl.ds(pl.multiple_of(dest * DH, DH), DH)
        sem = load_sems.at[dest]
        pltpu.make_async_copy(keys_ref.at[rows, cols], held.at[i, 0], sem).start()
        pltpu.make_async_copy(values_ref.at[rows, cols], held.at[i, 1], sem).start()
        return 0

    lax.fori_loop(0, MEMS * CAP, issue, 0, unroll=4)
    for dest in range(MEMS):
        mine = pl.ds(dest * CAP, CAP)
        pltpu.make_async_copy(out_ref.at[mine], held.at[mine], load_sems.at[dest]).wait()
        pltpu.make_async_copy(held.at[mine], out_ref.at[mine], store_sem).start()
    pltpu.make_async_copy(held, out_ref, store_sem).wait()


def serve(wanted, keys, values):
    hbm = pl.BlockSpec(memory_space=pl.ANY)
    return pl.pallas_call(
        serve_kernel,
        out_shape=jax.ShapeDtypeStruct((MEMS * CAP, 2, TILE, DH), BF16),
        in_specs=[pl.BlockSpec(memory_space=pltpu.SMEM), hbm, hbm],
        out_specs=hbm,
        scratch_shapes=[
            pltpu.VMEM((MEMS * CAP, 2, TILE, DH), BF16),
            pltpu.SemaphoreType.DMA((MEMS,)),
            pltpu.SemaphoreType.DMA(()),
        ],
        compiler_params=pltpu.CompilerParams(vmem_limit_bytes=48 * MIB),
        cost_estimate=pl.CostEstimate(flops=0, bytes_accessed=12 * MIB, transcendentals=0),
        name="serve",
    )(wanted, keys, values)


def local_kernel(
    tokens_ref, wq_ref, wk_ref, wv_ref, cot_ref, bias_ref,
    queries_ref, out_ref, dq_ref, mine_ref, other_ref, weights, total,
):
    step = pl.program_id(0)

    @pl.when(step == 0)
    def _():
        weights[:, :DH] = wq_ref[...]
        weights[:, DH : 2 * DH] = wk_ref[...]
        weights[:, 2 * DH :] = wv_ref[...]
        total[...] = jnp.zeros_like(total)

    x = tokens_ref[...]
    qkv = dot(x, weights[...]).astype(BF16)
    q, k, v = qkv[:, :DH], qkv[:, DH : 2 * DH], qkv[:, 2 * DH :]
    queries_ref[...] = q
    gate = gate_row(bias_ref)
    grad = ((1.0 - gate) * cot_ref[...].astype(F32)).astype(BF16)
    half = SEG // 2
    grad_k = []
    grad_v = []
    for part in range(2):
        rows = slice(part * half, (part + 1) * half)
        width = (part + 1) * half
        qs, gs, ks, vs = q[rows], grad[rows], k[:width], v[:width]
        scores = dot(qs, ks, NT) * SCALING
        keep = iota((half, width), 0) + part * half >= iota((half, width), 1)
        scores = jnp.where(keep, scores, -jnp.inf)
        raised = jnp.exp(scores - jnp.max(scores, axis=1, keepdims=True))
        probs = raised * (1.0 / jnp.sum(raised, axis=1, keepdims=True))
        rounded = probs.astype(BF16)
        out_ref[rows, :] = dot(rounded, vs)
        back = dot(gs, vs, NT)
        dscore = probs * (back - jnp.sum(back * probs, axis=1, keepdims=True)) * SCALING
        dround = dscore.astype(BF16)
        dq_ref[rows, :] = dot(dround, ks)
        grad_k.append(dot(dround, qs, TN))
        grad_v.append(dot(rounded, gs, TN))
    low = jnp.concatenate([grad_k[0] + grad_k[1][:half], grad_v[0] + grad_v[1][:half]], axis=1)
    high = jnp.concatenate([grad_k[1][half:], grad_v[1][half:]], axis=1)
    both = jnp.concatenate([low, high], axis=0).astype(BF16)
    total[...] += dot(x, both, TN)

    @pl.when(step == SEGS - 1)
    def _():
        me = lax.axis_index("dp")
        core = lax.rem(me, 2)
        for z in range(ZS):
            owner = lax.rem(me // 2 + z, ZS) * 2
            for part_ref, side in ((mine_ref, core), (other_ref, 1 - core)):
                at = pl.ds(pl.multiple_of((owner + side) * ROWS_OUT, ROWS_OUT), ROWS_OUT)
                part_ref[z] = total[at, :].astype(part_ref.dtype)


def local_part(tokens, w_query, w_key, w_value, cot, bias):
    seg = lambda width: pl.BlockSpec((SEG, width), lambda i: (i, 0))
    whole = pl.BlockSpec((D, DH), lambda i: (0, 0), pipeline_mode=pl.Buffered(1))
    fixed = pl.BlockSpec((ZS, ROWS_OUT, 2 * DH), lambda i: (0, 0, 0))
    return pl.pallas_call(
        local_kernel,
        grid=(SEGS,),
        out_shape=(
            jax.ShapeDtypeStruct((TOK, DH), BF16),
            jax.ShapeDtypeStruct((TOK, DH), F32),
            jax.ShapeDtypeStruct((TOK, DH), F32),
            jax.ShapeDtypeStruct((ZS, ROWS_OUT, 2 * DH), F32),
            jax.ShapeDtypeStruct((ZS, ROWS_OUT, 2 * DH), BF16),
        ),
        in_specs=[seg(D), whole, whole, whole, seg(DH), pl.BlockSpec(memory_space=pltpu.SMEM)],
        out_specs=(seg(DH), seg(DH), seg(DH), fixed, fixed),
        scratch_shapes=[pltpu.VMEM((D, 3 * DH), BF16), pltpu.VMEM((D, 2 * DH), F32)],
        compiler_params=pltpu.CompilerParams(
            dimension_semantics=("arbitrary",), vmem_limit_bytes=48 * MIB
        ),
        cost_estimate=pl.CostEstimate(
            flops=14_000_000_000, bytes_accessed=20 * MIB, transcendentals=1_600_000
        ),
        name="local",
    )(tokens, w_query, w_key, w_value, cot, bias)


CLASSES = ((2, 6), (4, 3), (8, 3))


def attend_all(members, tiles_n, refs):
    gate, tiles, queries_ref, cot_ref, outs, dqs = refs
    width = tiles_n * TILE
    at = [pl.ds(pl.multiple_of(block * QB, QB), QB) for block, _, _ in members]
    entries = [pl.ds(block * TOP, tiles_n) for block, _, _ in members]
    keys = [tiles[e, 0].reshape(width, DH) for e in entries]
    values = [tiles[e, 1].reshape(width, DH) for e in entries]
    up = [cot_ref[rows, :].astype(F32) for rows in at]
    queries = [queries_ref[rows, :] for rows in at]
    scores = [dot(k, q, NT) for k, q in zip(keys, queries)]
    back = [dot(v, (gate * u).astype(BF16), NT) for v, u in zip(values, up)]
    probs = []
    for s, (_, _, count) in zip(scores, members):
        s = jnp.where(iota((width, QB), 0) < count * TILE, s * SCALING, -jnp.inf)
        raised = jnp.exp(s - jnp.max(s, axis=0, keepdims=True))
        probs.append(raised * (1.0 / jnp.sum(raised, axis=0, keepdims=True)))
    out = [dot(p.astype(BF16), v, TN) for p, v in zip(probs, values)]
    dscore = [
        p * (b - jnp.sum(b * p, axis=0, keepdims=True)) * SCALING for p, b in zip(probs, back)
    ]
    dq = [dot(d.astype(BF16), k, TN) for d, k in zip(dscore, keys)]
    for rows, o, d in zip(at, out, dq):
        outs[rows, :] = o
        dqs[rows, :] = d


def memory_kernel(
    counts_ref, slot_ref, bias_ref, tiles_ref, queries_in, local_in, ldq_in, cot_in, tokens_ref,
    attended_out, mine_ref, other_ref, tiles, tokens, total, grads, gate_sum, lists, sizes,
    local_ref, ldq_ref, outs, dqs, queries_ref, cot_ref, attended_ref, sems, token_sems, row_sems,
    out_sems,
):
    pltpu.make_async_copy(queries_in, queries_ref, row_sems.at[2]).start()
    pltpu.make_async_copy(cot_in, cot_ref, row_sems.at[3]).start()

    def sort(block, _):
        count = counts_ref[0, block]

        def fetch(slot, _):
            entry = block * TOP + slot
            pltpu.make_async_copy(tiles_ref.at[slot_ref[0, entry]], tiles.at[entry], sems.at[entry]).start()
            return 0

        lax.fori_loop(0, count, fetch, 0)
        at = (count > 2).astype(jnp.int32) + (count > 4).astype(jnp.int32)
        place = sizes[at]
        lists[at, place] = block
        sizes[at] = place + 1

        def clear(slot, _):
            tiles[block * TOP + slot] = jnp.zeros((2, TILE, DH), BF16)
            return 0

        lax.fori_loop(count, lax.shift_left(2, at), clear, 0)
        return 0

    for at in range(len(CLASSES)):
        sizes[at] = 0
    lax.fori_loop(0, NQB, sort, 0)
    pltpu.make_async_copy(local_in, local_ref, row_sems.at[0]).start()
    pltpu.make_async_copy(ldq_in, ldq_ref, row_sems.at[1]).start()
    for part in range(SEGS):
        rows = pl.ds(part * SEG, SEG)
        pltpu.make_async_copy(tokens_ref.at[rows], tokens.at[rows], token_sems.at[part]).start()
    gate = gate_row(bias_ref)
    gate_sum[...] = jnp.zeros_like(gate_sum)
    pltpu.make_async_copy(queries_in, queries_ref, row_sems.at[2]).wait()
    pltpu.make_async_copy(cot_in, cot_ref, row_sems.at[3]).wait()
    for at, (tiles_n, group) in enumerate(CLASSES):

        def batch(i, _, at=at, tiles_n=tiles_n, group=group):
            members = []
            for k in range(group):
                valid = i * group + k < sizes[at]
                block = lists[at, jnp.minimum(i * group + k, sizes[at] - 1)]
                count = counts_ref[0, block]
                members.append((block, valid, count))

                def arrive(slot, _):
                    entry = block * TOP + slot
                    pltpu.make_async_copy(
                        tiles_ref.at[0], tiles.at[entry], sems.at[entry]
                    ).wait()
                    return 0

                lax.fori_loop(0, jnp.where(valid, count, 0), arrive, 0)
            attend_all(members, tiles_n, (gate, tiles, queries_ref, cot_ref, outs, dqs))
            return 0

        lax.fori_loop(0, pl.cdiv(sizes[at], group), batch, 0)
    pltpu.make_async_copy(local_in, local_ref, row_sems.at[0]).wait()
    pltpu.make_async_copy(ldq_in, ldq_ref, row_sems.at[1]).wait()
    for part in range(SEGS):
        rows = pl.ds(part * SEG, SEG)
        local = local_ref[rows, :]
        out = outs[rows, :]
        attended_ref[rows, :] = (gate * out + (1.0 - gate) * local).astype(BF16)
        pltpu.make_async_copy(attended_ref.at[rows], attended_out.at[rows], out_sems.at[part]).start()
        terms = cot_ref[rows, :].astype(F32) * (out - local)
        gate_sum[...] += jnp.sum(terms, axis=0, keepdims=True)
        grads[rows, :] = (dqs[rows, :] + ldq_ref[rows, :]).astype(BF16)
    for part in range(SEGS):
        rows = pl.ds(part * SEG, SEG)
        pltpu.make_async_copy(tokens_ref.at[rows], tokens.at[rows], token_sems.at[part]).wait()
        term = dot(grads[rows, :], tokens[rows, :], TN)
        if part == 0:
            total[...] = term
        else:
            total[...] += term
    me = lax.axis_index("dp")
    core = lax.rem(me, 2)
    extra = split_gate(gate_sum[...])
    for step in range(ZS):
        owner = lax.rem(me // 2 + step, ZS) * 2
        for out_ref, side in ((mine_ref, core), (other_ref, 1 - core)):
            cols = pl.ds(pl.multiple_of((owner + side) * ROWS_OUT, ROWS_OUT), ROWS_OUT)
            out_ref[step, :ROWS_OUT, :] = total[:, cols].T.astype(out_ref.dtype)
        mine_ref[step, ROWS_OUT:, :] = extra[0]
        other_ref[step, ROWS_OUT:, :] = extra[1].astype(BF16)
    for part in range(SEGS):
        rows = pl.ds(part * SEG, SEG)
        pltpu.make_async_copy(attended_ref.at[rows], attended_out.at[rows], out_sems.at[part]).wait()


def split_gate(term):
    high = term.astype(BF16).astype(F32)
    mid = (term - high).astype(BF16).astype(F32)
    low = term - high - mid
    at = iota((GATE_ROWS, DH), 0)
    spread = lambda row: jnp.broadcast_to(row, (GATE_ROWS, DH))
    parts = []
    for first in (0, 3):
        row = jnp.where(at == first, spread(high), jnp.where(at == first + 1, spread(mid), spread(low)))
        parts.append(jnp.where((at >= first) & (at < first + 3), row, 0.0))
    return parts


def memory_part(counts, slots, bias, tiles, queries, local, ldq, cot, tokens):
    smem = pl.BlockSpec(memory_space=pltpu.SMEM)
    vmem = pl.BlockSpec(memory_space=pltpu.VMEM)
    hbm = pl.BlockSpec(memory_space=pl.ANY)
    rows = ROWS_OUT + GATE_ROWS
    return pl.pallas_call(
        memory_kernel,
        out_shape=(
            jax.ShapeDtypeStruct((TOK, DH), BF16),
            jax.ShapeDtypeStruct((ZS, rows, DH), F32),
            jax.ShapeDtypeStruct((ZS, rows, DH), BF16),
        ),
        in_specs=[smem] * 3 + [hbm] * 6,
        out_specs=(hbm, vmem, vmem),
        scratch_shapes=[
            pltpu.VMEM((ENTRIES, 2, TILE, DH), BF16),
            pltpu.VMEM((TOK, D), BF16),
            pltpu.VMEM((DH, D), F32),
            pltpu.VMEM((TOK, DH), BF16),
            pltpu.VMEM((1, DH), F32),
            pltpu.SMEM((len(CLASSES), 32), jnp.int32),
            pltpu.SMEM((len(CLASSES),), jnp.int32),
            pltpu.VMEM((TOK, DH), F32),
            pltpu.VMEM((TOK, DH), F32),
            pltpu.VMEM((TOK, DH), F32),
            pltpu.VMEM((TOK, DH), F32),
            pltpu.VMEM((TOK, DH), BF16),
            pltpu.VMEM((TOK, DH), BF16),
            pltpu.VMEM((TOK, DH), BF16),
            pltpu.SemaphoreType.DMA((ENTRIES,)),
            pltpu.SemaphoreType.DMA((SEGS,)),
            pltpu.SemaphoreType.DMA((4,)),
            pltpu.SemaphoreType.DMA((SEGS,)),
        ],
        compiler_params=pltpu.CompilerParams(vmem_limit_bytes=59 * MIB),
        cost_estimate=pl.CostEstimate(
            flops=8_000_000_000, bytes_accessed=24 * MIB, transcendentals=1_600_000
        ),
        name="memory",
    )(counts, slots, bias, tiles, queries, local, ldq, cot, tokens)


def swap_cores(array):
    return lax.ppermute(array, "dp", [(i, i ^ 1) for i in range(2 * ZS)])


def along_z(array, step):
    return lax.ppermute(array, "dp", [(i, (i + 2 * step) % (2 * ZS)) for i in range(2 * ZS)])


def reduce_docs(mine, other):
    got = swap_cores(other)
    parts = [mine[0] + got[0].astype(F32)]
    for step in range(1, ZS):
        both = (mine[step] + got[step].astype(F32)).astype(BF16)
        parts.append(along_z(both, step).astype(F32))
    return parts


def exchange(array, axis):
    return lax.all_to_all(array, axis, split_axis=0, concat_axis=0, tiled=True)


def on_device(
    tokens,
    w_query,
    w_key,
    w_value,
    gate_bias,
    memory_keys,
    memory_values,
    retrieval_ids,
    retrieval_counts,
    cotangent,
):
    hidden = tokens[0]
    cot = cotangent[0]
    counts = retrieval_counts.reshape(1, NQB)
    table, slots = make_requests(retrieval_ids.reshape(NQB, TOP).T, counts)
    wanted = exchange(table, "mem")
    sent = serve(wanted, memory_keys[0], memory_values[0])
    hidden, sent = lax.optimization_barrier((hidden, sent))
    tiles = exchange(sent, "mem")
    queries, local, ldq, mine, other = local_part(hidden, w_query, w_key, w_value, cot, gate_bias)
    sum_kv = sum(reduce_docs(mine, other))
    share_k, share_v = sum_kv[:, :DH], sum_kv[:, DH:]
    counts, share_k, share_v = lax.optimization_barrier((counts, share_k, share_v))
    attended, mine, other = memory_part(
        counts, slots, gate_bias, tiles, queries, local, ldq, cot, hidden
    )
    parts = reduce_docs(mine, other)
    share_q = sum(part[:ROWS_OUT] for part in parts)
    gate_rows = sum(part[ROWS_OUT : ROWS_OUT + 6] for part in parts)
    gate = jax.nn.sigmoid(gate_bias)
    gate_total = jnp.sum(gate_rows) * gate * (1.0 - gate)
    return (attended[None], share_q, share_k, share_v, gate_total)


def solution(mesh):
    return jax.shard_map(
        on_device,
        mesh=mesh,
        in_specs=(
            P("dp", None, None),
            P(None, "mem"),
            P(None, "mem"),
            P(None, "mem"),
            P("mem"),
            P("dp", "mem", None),
            P("dp", "mem", None),
            P("dp", "mem", None, None),
            P("dp", "mem", None),
            P("dp", None, "mem"),
        ),
        out_specs=(P("dp", None, "mem"), P("dp", "mem"), P("dp", "mem"), P("dp", "mem"), P("mem")),
        check_vma=False,
    )
```

```python
import functools

import jax
import jax.numpy as jnp
from jax import lax
from jax.experimental import pallas as pl
from jax.experimental.pallas import tpu as pltpu
from jax.sharding import PartitionSpec as P

DH = 128
SEG = 512
QB = 128
TILE = 64
TOP = 8
SEGS = 6
TILES_DEV = 24
TOK = 3072
NQB = 24
CAP = 12
MEMS = 16
D = 2048
ENTRIES = NQB * TOP
SCALING = DH ** (-0.5)
ROWS_OUT = D // 8
GATE_ROWS = 16
ZS = 4
F32 = jnp.float32
BF16 = jnp.bfloat16
MIB = 1 << 20

NT = (((1,), (1,)), ((), ()))
TN = (((0,), (0,)), ((), ()))


def dot(a, b, dims=(((1,), (0,)), ((), ()))):
    return lax.dot_general(a, b, dims, preferred_element_type=F32)


def iota(shape, dim):
    return lax.broadcasted_iota(jnp.int32, shape, dim)


def gate_row(bias_ref):
    return 1.0 / (1.0 + jnp.exp(-jnp.full((1, DH), bias_ref[0], F32)))


def request_kernel(ids_ref, counts_ref, table_ref, slot_ref):
    ids = ids_ref[...]
    owner = (ids // TILES_DEV).astype(F32)
    local = (ids % TILES_DEV).astype(F32)
    counts = counts_ref[...].astype(F32)
    by_block = (iota((ENTRIES, NQB), 0) // TOP == iota((ENTRIES, NQB), 1)).astype(F32)
    pick = (iota((ENTRIES, TOP), 0) % TOP == iota((ENTRIES, TOP), 1)).astype(F32)
    owner_col = jnp.sum(dot(by_block, owner, NT) * pick, axis=1, keepdims=True)
    local_col = jnp.sum(dot(by_block, local, NT) * pick, axis=1, keepdims=True)
    count_col = jnp.sum(by_block * counts, axis=1, keepdims=True)
    slot_col = (iota((ENTRIES, 1), 0) % TOP).astype(F32)
    owner_col = jnp.where(slot_col < count_col, owner_col, float(MEMS))
    of_block = (iota((NQB, ENTRIES), 1) // TOP == iota((NQB, ENTRIES), 0)).astype(F32)
    of_slot = (iota((TOP, ENTRIES), 1) % TOP == iota((TOP, ENTRIES), 0)).astype(F32)
    owner_row = jnp.sum(dot(owner, of_slot, TN) * of_block, axis=0, keepdims=True)
    count_row = dot(jnp.broadcast_to(counts, (8, NQB)), of_block)[:1]
    slot_row = (iota((1, ENTRIES), 1) % TOP).astype(F32)
    owner_row = jnp.where(slot_row < count_row, owner_row, float(MEMS))
    same = owner_col == owner_row
    first = iota((ENTRIES, ENTRIES), 0)
    second = iota((ENTRIES, ENTRIES), 1)
    rank_col = jnp.sum((same & (second < first)).astype(F32), axis=1, keepdims=True)
    rank_row = jnp.sum((same & (first < second)).astype(F32), axis=0, keepdims=True)
    sends = (owner_row == iota((MEMS, ENTRIES), 0).astype(F32)).astype(F32)
    place = jnp.where(rank_col == iota((ENTRIES, 128), 1).astype(F32), local_col, 0.0)
    table_ref[...] = dot(sends, place).astype(jnp.int32)
    slot_ref[...] = jnp.clip(owner_row * CAP + rank_row, 0.0, float(MEMS * CAP - 1)).astype(jnp.int32)


def make_requests(ids, counts):
    return pl.pallas_call(
        request_kernel,
        out_shape=(
            jax.ShapeDtypeStruct((MEMS, 128), jnp.int32),
            jax.ShapeDtypeStruct((1, ENTRIES), jnp.int32),
        ),
        name="request",
    )(ids, counts)


def serve_kernel(wanted_ref, keys_ref, values_ref, out_ref, held, load_sems, store_sem):
    def store(dest):
        mine = pl.ds(dest * CAP, CAP)
        pltpu.make_async_copy(out_ref.at[mine], held.at[mine], load_sems.at[dest]).wait()
        pltpu.make_async_copy(held.at[mine], out_ref.at[mine], store_sem).start()

    def issue(dest, _):
        cols = pl.ds(pl.multiple_of(dest * DH, DH), DH)
        sem = load_sems.at[dest]
        for rank in range(CAP):
            rows = pl.ds(pl.multiple_of(wanted_ref[dest, rank] * TILE, TILE), TILE)
            slot = held.at[dest * CAP + rank]
            pltpu.make_async_copy(keys_ref.at[rows, cols], slot.at[0], sem).start()
            pltpu.make_async_copy(values_ref.at[rows, cols], slot.at[1], sem).start()

        return 0

    lax.fori_loop(0, MEMS, issue, 0)
    for dest in range(MEMS):
        store(dest)
    pltpu.make_async_copy(held, out_ref, store_sem).wait()


def serve(wanted, keys, values):
    hbm = pl.BlockSpec(memory_space=pl.ANY)
    return pl.pallas_call(
        serve_kernel,
        out_shape=jax.ShapeDtypeStruct((MEMS * CAP, 2, TILE, DH), BF16),
        in_specs=[pl.BlockSpec(memory_space=pltpu.SMEM), hbm, hbm],
        out_specs=hbm,
        scratch_shapes=[
            pltpu.VMEM((MEMS * CAP, 2, TILE, DH), BF16),
            pltpu.SemaphoreType.DMA((MEMS,)),
            pltpu.SemaphoreType.DMA(()),
        ],
        compiler_params=pltpu.CompilerParams(vmem_limit_bytes=48 * MIB),
        cost_estimate=pl.CostEstimate(flops=0, bytes_accessed=12 * MIB, transcendentals=0),
        name="serve",
    )(wanted, keys, values)


def local_kernel(
    tokens_ref, wq_ref, wk_ref, wv_ref, cot_ref, bias_ref,
    queries_ref, out_ref, dq_ref, mine_ref, other_ref, weights, total,
):
    step = pl.program_id(0)

    @pl.when(step == 0)
    def _():
        weights[:, :DH] = wq_ref[...]
        weights[:, DH : 2 * DH] = wk_ref[...]
        weights[:, 2 * DH :] = wv_ref[...]
        total[...] = jnp.zeros_like(total)

    x = tokens_ref[...]
    qkv = dot(x, weights[...]).astype(BF16)
    q, k, v = qkv[:, :DH], qkv[:, DH : 2 * DH], qkv[:, 2 * DH :]
    queries_ref[...] = q
    gate = gate_row(bias_ref)
    grad = ((1.0 - gate) * cot_ref[...].astype(F32)).astype(BF16)
    half = SEG // 2
    grad_k = []
    grad_v = []
    for part in range(2):
        rows = slice(part * half, (part + 1) * half)
        width = (part + 1) * half
        qs, gs, ks, vs = q[rows], grad[rows], k[:width], v[:width]
        scores = dot(qs, ks, NT) * SCALING
        keep = iota((half, width), 0) + part * half >= iota((half, width), 1)
        scores = jnp.where(keep, scores, -jnp.inf)
        raised = jnp.exp(scores - jnp.max(scores, axis=1, keepdims=True))
        probs = raised * (1.0 / jnp.sum(raised, axis=1, keepdims=True))
        rounded = probs.astype(BF16)
        out_ref[rows, :] = dot(rounded, vs)
        back = dot(gs, vs, NT)
        dscore = probs * (back - jnp.sum(back * probs, axis=1, keepdims=True)) * SCALING
        dround = dscore.astype(BF16)
        dq_ref[rows, :] = dot(dround, ks)
        grad_k.append(dot(dround, qs, TN))
        grad_v.append(dot(rounded, gs, TN))
    low = jnp.concatenate([grad_k[0] + grad_k[1][:half], grad_v[0] + grad_v[1][:half]], axis=1)
    high = jnp.concatenate([grad_k[1][half:], grad_v[1][half:]], axis=1)
    both = jnp.concatenate([low, high], axis=0).astype(BF16)
    total[...] += dot(x, both, TN)

    @pl.when(step == SEGS - 1)
    def _():
        me = lax.axis_index("dp")
        core = lax.rem(me, 2)
        for z in range(ZS):
            owner = lax.rem(me // 2 + z, ZS) * 2
            for part_ref, side in ((mine_ref, core), (other_ref, 1 - core)):
                at = pl.ds(pl.multiple_of((owner + side) * ROWS_OUT, ROWS_OUT), ROWS_OUT)
                part_ref[z] = total[at, :].astype(part_ref.dtype)


def local_part(tokens, w_query, w_key, w_value, cot, bias):
    seg = lambda width: pl.BlockSpec((SEG, width), lambda i: (i, 0))
    whole = pl.BlockSpec((D, DH), lambda i: (0, 0), pipeline_mode=pl.Buffered(1))
    fixed = pl.BlockSpec((ZS, ROWS_OUT, 2 * DH), lambda i: (0, 0, 0))
    return pl.pallas_call(
        local_kernel,
        grid=(SEGS,),
        out_shape=(
            jax.ShapeDtypeStruct((TOK, DH), BF16),
            jax.ShapeDtypeStruct((TOK, DH), F32),
            jax.ShapeDtypeStruct((TOK, DH), F32),
            jax.ShapeDtypeStruct((ZS, ROWS_OUT, 2 * DH), F32),
            jax.ShapeDtypeStruct((ZS, ROWS_OUT, 2 * DH), BF16),
        ),
        in_specs=[seg(D), whole, whole, whole, seg(DH), pl.BlockSpec(memory_space=pltpu.SMEM)],
        out_specs=(seg(DH), seg(DH), seg(DH), fixed, fixed),
        scratch_shapes=[pltpu.VMEM((D, 3 * DH), BF16), pltpu.VMEM((D, 2 * DH), F32)],
        compiler_params=pltpu.CompilerParams(
            dimension_semantics=("arbitrary",), vmem_limit_bytes=48 * MIB
        ),
        cost_estimate=pl.CostEstimate(
            flops=14_000_000_000, bytes_accessed=20 * MIB, transcendentals=1_600_000
        ),
        name="local",
    )(tokens, w_query, w_key, w_value, cot, bias)


CLASSES = ((2, 6), (4, 3), (8, 6))


def attend_all(members, tiles_n, refs):
    gate, tiles, queries_ref, cot_ref, outs, dqs = refs
    width = tiles_n * TILE
    at = [pl.ds(pl.multiple_of(block * QB, QB), QB) for block, _, _ in members]
    entries = [pl.ds(block * TOP, tiles_n) for block, _, _ in members]
    keys = [tiles[e, 0].reshape(width, DH) for e in entries]
    values = [tiles[e, 1].reshape(width, DH) for e in entries]
    up = [cot_ref[rows, :].astype(F32) for rows in at]
    queries = [queries_ref[rows, :] for rows in at]
    scores = [dot(k, q, NT) for k, q in zip(keys, queries)]
    back = [dot(v, (gate * u).astype(BF16), NT) for v, u in zip(values, up)]
    probs = []
    for s, (_, _, count) in zip(scores, members):
        s = jnp.where(iota((width, QB), 0) < count * TILE, s * SCALING, -jnp.inf)
        raised = jnp.exp(s - jnp.max(s, axis=0, keepdims=True))
        probs.append(raised * (1.0 / jnp.sum(raised, axis=0, keepdims=True)))
    out = [dot(p.astype(BF16), v, TN) for p, v in zip(probs, values)]
    dscore = [
        p * (b - jnp.sum(b * p, axis=0, keepdims=True)) * SCALING for p, b in zip(probs, back)
    ]
    dq = [dot(d.astype(BF16), k, TN) for d, k in zip(dscore, keys)]
    for rows, o, d in zip(at, out, dq):
        outs[rows, :] = o
        dqs[rows, :] = d


def memory_kernel(
    counts_ref, slot_ref, bias_ref, tiles_ref, queries_in, local_in, ldq_in, cot_in, tokens_ref,
    attended_out, mine_ref, other_ref, tiles, tokens, total, grads, gate_sum, lists, sizes,
    local_ref, ldq_ref, outs, dqs, queries_ref, cot_ref, attended_ref, sems, token_sems, row_sems,
    out_sems,
):
    pltpu.make_async_copy(queries_in, queries_ref, row_sems.at[2]).start()
    pltpu.make_async_copy(cot_in, cot_ref, row_sems.at[3]).start()

    def sort(block, _):
        count = counts_ref[0, block]

        def fetch(slot, _):
            entry = block * TOP + slot
            pltpu.make_async_copy(tiles_ref.at[slot_ref[0, entry]], tiles.at[entry], sems.at[entry]).start()
            return 0

        lax.fori_loop(0, count, fetch, 0)
        at = (count > 2).astype(jnp.int32) + (count > 4).astype(jnp.int32)
        place = sizes[at]
        lists[at, place] = block
        sizes[at] = place + 1

        def clear(slot, _):
            tiles[block * TOP + slot] = jnp.zeros((2, TILE, DH), BF16)
            return 0

        lax.fori_loop(count, lax.shift_left(2, at), clear, 0)
        return 0

    for at in range(len(CLASSES)):
        sizes[at] = 0
    lax.fori_loop(0, NQB, sort, 0)
    pltpu.make_async_copy(local_in, local_ref, row_sems.at[0]).start()
    pltpu.make_async_copy(ldq_in, ldq_ref, row_sems.at[1]).start()
    for part in range(SEGS):
        rows = pl.ds(part * SEG, SEG)
        pltpu.make_async_copy(tokens_ref.at[rows], tokens.at[rows], token_sems.at[part]).start()
    gate = gate_row(bias_ref)
    gate_sum[...] = jnp.zeros_like(gate_sum)
    pltpu.make_async_copy(queries_in, queries_ref, row_sems.at[2]).wait()
    pltpu.make_async_copy(cot_in, cot_ref, row_sems.at[3]).wait()
    for at, (tiles_n, group) in enumerate(CLASSES):

        def batch(i, _, at=at, tiles_n=tiles_n, group=group):
            members = []
            for k in range(group):
                valid = i * group + k < sizes[at]
                block = lists[at, jnp.minimum(i * group + k, sizes[at] - 1)]
                count = counts_ref[0, block]
                members.append((block, valid, count))

                def arrive(slot, _):
                    entry = block * TOP + slot
                    pltpu.make_async_copy(
                        tiles_ref.at[0], tiles.at[entry], sems.at[entry]
                    ).wait()
                    return 0

                lax.fori_loop(0, jnp.where(valid, count, 0), arrive, 0)
            attend_all(members, tiles_n, (gate, tiles, queries_ref, cot_ref, outs, dqs))
            return 0

        lax.fori_loop(0, pl.cdiv(sizes[at], group), batch, 0)
    pltpu.make_async_copy(local_in, local_ref, row_sems.at[0]).wait()
    pltpu.make_async_copy(ldq_in, ldq_ref, row_sems.at[1]).wait()
    for part in range(SEGS):
        rows = pl.ds(part * SEG, SEG)
        local = local_ref[rows, :]
        out = outs[rows, :]
        attended_ref[rows, :] = (gate * out + (1.0 - gate) * local).astype(BF16)
        pltpu.make_async_copy(attended_ref.at[rows], attended_out.at[rows], out_sems.at[part]).start()
        terms = cot_ref[rows, :].astype(F32) * (out - local)
        gate_sum[...] += jnp.sum(terms, axis=0, keepdims=True)
        grads[rows, :] = (dqs[rows, :] + ldq_ref[rows, :]).astype(BF16)
    for part in range(SEGS):
        rows = pl.ds(part * SEG, SEG)
        pltpu.make_async_copy(tokens_ref.at[rows], tokens.at[rows], token_sems.at[part]).wait()
        term = dot(grads[rows, :], tokens[rows, :], TN)
        if part == 0:
            total[...] = term
        else:
            total[...] += term
    me = lax.axis_index("dp")
    core = lax.rem(me, 2)
    extra = split_gate(gate_sum[...])
    for step in range(ZS):
        owner = lax.rem(me // 2 + step, ZS) * 2
        for out_ref, side in ((mine_ref, core), (other_ref, 1 - core)):
            cols = pl.ds(pl.multiple_of((owner + side) * ROWS_OUT, ROWS_OUT), ROWS_OUT)
            out_ref[step, :ROWS_OUT, :] = total[:, cols].T.astype(out_ref.dtype)
        mine_ref[step, ROWS_OUT:, :] = extra[0]
        other_ref[step, ROWS_OUT:, :] = extra[1].astype(BF16)
    for part in range(SEGS):
        rows = pl.ds(part * SEG, SEG)
        pltpu.make_async_copy(attended_ref.at[rows], attended_out.at[rows], out_sems.at[part]).wait()


def split_gate(term):
    high = term.astype(BF16).astype(F32)
    mid = (term - high).astype(BF16).astype(F32)
    low = term - high - mid
    at = iota((GATE_ROWS, DH), 0)
    spread = lambda row: jnp.broadcast_to(row, (GATE_ROWS, DH))
    parts = []
    for first in (0, 3):
        row = jnp.where(at == first, spread(high), jnp.where(at == first + 1, spread(mid), spread(low)))
        parts.append(jnp.where((at >= first) & (at < first + 3), row, 0.0))
    return parts


def memory_part(counts, slots, bias, tiles, queries, local, ldq, cot, tokens):
    smem = pl.BlockSpec(memory_space=pltpu.SMEM)
    vmem = pl.BlockSpec(memory_space=pltpu.VMEM)
    hbm = pl.BlockSpec(memory_space=pl.ANY)
    rows = ROWS_OUT + GATE_ROWS
    return pl.pallas_call(
        memory_kernel,
        out_shape=(
            jax.ShapeDtypeStruct((TOK, DH), BF16),
            jax.ShapeDtypeStruct((ZS, rows, DH), F32),
            jax.ShapeDtypeStruct((ZS, rows, DH), BF16),
        ),
        in_specs=[smem] * 3 + [hbm] * 6,
        out_specs=(hbm, vmem, vmem),
        scratch_shapes=[
            pltpu.VMEM((ENTRIES, 2, TILE, DH), BF16),
            pltpu.VMEM((TOK, D), BF16),
            pltpu.VMEM((DH, D), F32),
            pltpu.VMEM((TOK, DH), BF16),
            pltpu.VMEM((1, DH), F32),
            pltpu.SMEM((len(CLASSES), 32), jnp.int32),
            pltpu.SMEM((len(CLASSES),), jnp.int32),
            pltpu.VMEM((TOK, DH), F32),
            pltpu.VMEM((TOK, DH), F32),
            pltpu.VMEM((TOK, DH), F32),
            pltpu.VMEM((TOK, DH), F32),
            pltpu.VMEM((TOK, DH), BF16),
            pltpu.VMEM((TOK, DH), BF16),
            pltpu.VMEM((TOK, DH), BF16),
            pltpu.SemaphoreType.DMA((ENTRIES,)),
            pltpu.SemaphoreType.DMA((SEGS,)),
            pltpu.SemaphoreType.DMA((4,)),
            pltpu.SemaphoreType.DMA((SEGS,)),
        ],
        compiler_params=pltpu.CompilerParams(vmem_limit_bytes=59 * MIB),
        cost_estimate=pl.CostEstimate(
            flops=8_000_000_000, bytes_accessed=24 * MIB, transcendentals=1_600_000
        ),
        name="memory",
    )(counts, slots, bias, tiles, queries, local, ldq, cot, tokens)


def swap_cores(array):
    return lax.ppermute(array, "dp", [(i, i ^ 1) for i in range(2 * ZS)])


def along_z(array, step):
    return lax.ppermute(array, "dp", [(i, (i + 2 * step) % (2 * ZS)) for i in range(2 * ZS)])


def reduce_docs(mine, other):
    got = swap_cores(other)
    parts = [mine[0] + got[0].astype(F32)]
    for step in range(1, ZS):
        both = (mine[step] + got[step].astype(F32)).astype(BF16)
        parts.append(along_z(both, step).astype(F32))
    return parts


def exchange(array, axis):
    return lax.all_to_all(array, axis, split_axis=0, concat_axis=0, tiled=True)


def on_device(
    tokens,
    w_query,
    w_key,
    w_value,
    gate_bias,
    memory_keys,
    memory_values,
    retrieval_ids,
    retrieval_counts,
    cotangent,
):
    hidden = tokens[0]
    cot = cotangent[0]
    counts = retrieval_counts.reshape(1, NQB)
    table, slots = make_requests(retrieval_ids.reshape(NQB, TOP).T, counts)
    wanted = exchange(table, "mem")
    sent = serve(wanted, memory_keys[0], memory_values[0])
    hidden, sent = lax.optimization_barrier((hidden, sent))
    tiles = exchange(sent, "mem")
    queries, local, ldq, mine, other = local_part(hidden, w_query, w_key, w_value, cot, gate_bias)
    sum_kv = sum(reduce_docs(mine, other))
    share_k, share_v = sum_kv[:, :DH], sum_kv[:, DH:]
    counts, share_k, share_v = lax.optimization_barrier((counts, share_k, share_v))
    attended, mine, other = memory_part(
        counts, slots, gate_bias, tiles, queries, local, ldq, cot, hidden
    )
    parts = reduce_docs(mine, other)
    share_q = sum(part[:ROWS_OUT] for part in parts)
    gate_rows = sum(part[ROWS_OUT : ROWS_OUT + 6] for part in parts)
    gate = jax.nn.sigmoid(gate_bias)
    gate_total = jnp.sum(gate_rows) * gate * (1.0 - gate)
    return (attended[None], share_q, share_k, share_v, gate_total)


def solution(mesh):
    return jax.shard_map(
        on_device,
        mesh=mesh,
        in_specs=(
            P("dp", None, None),
            P(None, "mem"),
            P(None, "mem"),
            P(None, "mem"),
            P("mem"),
            P("dp", "mem", None),
            P("dp", "mem", None),
            P("dp", "mem", None, None),
            P("dp", "mem", None),
            P("dp", None, "mem"),
        ),
        out_specs=(P("dp", None, "mem"), P("dp", "mem"), P("dp", "mem"), P("dp", "mem"), P("mem")),
        check_vma=False,
    )
```

```python
import functools

import jax
import jax.numpy as jnp
from jax import lax
from jax.experimental import pallas as pl
from jax.experimental.pallas import tpu as pltpu
from jax.sharding import PartitionSpec as P

DH = 128
SEG = 512
QB = 128
TILE = 64
TOP = 8
SEGS = 6
TILES_DEV = 24
TOK = 3072
NQB = 24
CAP = 12
MEMS = 16
D = 2048
ENTRIES = NQB * TOP
SCALING = DH ** (-0.5)
ROWS_OUT = D // 8
GATE_ROWS = 16
ZS = 4
F32 = jnp.float32
BF16 = jnp.bfloat16
MIB = 1 << 20

NT = (((1,), (1,)), ((), ()))
TN = (((0,), (0,)), ((), ()))


def dot(a, b, dims=(((1,), (0,)), ((), ()))):
    return lax.dot_general(a, b, dims, preferred_element_type=F32)


def iota(shape, dim):
    return lax.broadcasted_iota(jnp.int32, shape, dim)


def gate_row(bias_ref):
    return 1.0 / (1.0 + jnp.exp(-jnp.full((1, DH), bias_ref[0], F32)))


def request_kernel(ids_ref, counts_ref, table_ref, slot_ref):
    ids = ids_ref[...]
    owner = (ids // TILES_DEV).astype(F32)
    local = (ids % TILES_DEV).astype(F32)
    counts = counts_ref[...].astype(F32)
    by_block = (iota((ENTRIES, NQB), 0) // TOP == iota((ENTRIES, NQB), 1)).astype(F32)
    pick = (iota((ENTRIES, TOP), 0) % TOP == iota((ENTRIES, TOP), 1)).astype(F32)
    owner_col = jnp.sum(dot(by_block, owner, NT) * pick, axis=1, keepdims=True)
    local_col = jnp.sum(dot(by_block, local, NT) * pick, axis=1, keepdims=True)
    count_col = jnp.sum(by_block * counts, axis=1, keepdims=True)
    slot_col = (iota((ENTRIES, 1), 0) % TOP).astype(F32)
    owner_col = jnp.where(slot_col < count_col, owner_col, float(MEMS))
    of_block = (iota((NQB, ENTRIES), 1) // TOP == iota((NQB, ENTRIES), 0)).astype(F32)
    of_slot = (iota((TOP, ENTRIES), 1) % TOP == iota((TOP, ENTRIES), 0)).astype(F32)
    owner_row = jnp.sum(dot(owner, of_slot, TN) * of_block, axis=0, keepdims=True)
    count_row = dot(jnp.broadcast_to(counts, (8, NQB)), of_block)[:1]
    slot_row = (iota((1, ENTRIES), 1) % TOP).astype(F32)
    owner_row = jnp.where(slot_row < count_row, owner_row, float(MEMS))
    same = owner_col == owner_row
    first = iota((ENTRIES, ENTRIES), 0)
    second = iota((ENTRIES, ENTRIES), 1)
    rank_col = jnp.sum((same & (second < first)).astype(F32), axis=1, keepdims=True)
    rank_row = jnp.sum((same & (first < second)).astype(F32), axis=0, keepdims=True)
    sends = (owner_row == iota((MEMS, ENTRIES), 0).astype(F32)).astype(F32)
    place = jnp.where(rank_col == iota((ENTRIES, 128), 1).astype(F32), local_col, 0.0)
    table_ref[...] = dot(sends, place).astype(jnp.int32)
    slot_ref[...] = jnp.clip(owner_row * CAP + rank_row, 0.0, float(MEMS * CAP - 1)).astype(jnp.int32)


def make_requests(ids, counts):
    return pl.pallas_call(
        request_kernel,
        out_shape=(
            jax.ShapeDtypeStruct((MEMS, 128), jnp.int32),
            jax.ShapeDtypeStruct((1, ENTRIES), jnp.int32),
        ),
        name="request",
    )(ids, counts)


def serve_kernel(wanted_ref, keys_ref, values_ref, out_ref, held, load_sems, store_sem):
    def store(dest):
        mine = pl.ds(dest * CAP, CAP)
        pltpu.make_async_copy(out_ref.at[mine], held.at[mine], load_sems.at[dest]).wait()
        pltpu.make_async_copy(held.at[mine], out_ref.at[mine], store_sem).start()

    def issue(dest, _):
        cols = pl.ds(pl.multiple_of(dest * DH, DH), DH)
        sem = load_sems.at[dest]
        for rank in range(CAP):
            rows = pl.ds(pl.multiple_of(wanted_ref[dest, rank] * TILE, TILE), TILE)
            slot = held.at[dest * CAP + rank]
            pltpu.make_async_copy(keys_ref.at[rows, cols], slot.at[0], sem).start()
            pltpu.make_async_copy(values_ref.at[rows, cols], slot.at[1], sem).start()

        return 0

    lax.fori_loop(0, MEMS, issue, 0, unroll=2)
    for dest in range(MEMS):
        store(dest)
    pltpu.make_async_copy(held, out_ref, store_sem).wait()


def serve(wanted, keys, values):
    hbm = pl.BlockSpec(memory_space=pl.ANY)
    return pl.pallas_call(
        serve_kernel,
        out_shape=jax.ShapeDtypeStruct((MEMS * CAP, 2, TILE, DH), BF16),
        in_specs=[pl.BlockSpec(memory_space=pltpu.SMEM), hbm, hbm],
        out_specs=hbm,
        scratch_shapes=[
            pltpu.VMEM((MEMS * CAP, 2, TILE, DH), BF16),
            pltpu.SemaphoreType.DMA((MEMS,)),
            pltpu.SemaphoreType.DMA(()),
        ],
        compiler_params=pltpu.CompilerParams(vmem_limit_bytes=48 * MIB),
        cost_estimate=pl.CostEstimate(flops=0, bytes_accessed=12 * MIB, transcendentals=0),
        name="serve",
    )(wanted, keys, values)


def local_kernel(
    tokens_ref, wq_ref, wk_ref, wv_ref, cot_ref, bias_ref,
    queries_ref, out_ref, dq_ref, mine_ref, other_ref, weights, total,
):
    step = pl.program_id(0)

    @pl.when(step == 0)
    def _():
        weights[:, :DH] = wq_ref[...]
        weights[:, DH : 2 * DH] = wk_ref[...]
        weights[:, 2 * DH :] = wv_ref[...]
        total[...] = jnp.zeros_like(total)

    x = tokens_ref[...]
    qkv = dot(x, weights[...]).astype(BF16)
    q, k, v = qkv[:, :DH], qkv[:, DH : 2 * DH], qkv[:, 2 * DH :]
    queries_ref[...] = q
    gate = gate_row(bias_ref)
    grad = ((1.0 - gate) * cot_ref[...].astype(F32)).astype(BF16)
    half = SEG // 2
    grad_k = []
    grad_v = []
    for part in range(2):
        rows = slice(part * half, (part + 1) * half)
        width = (part + 1) * half
        qs, gs, ks, vs = q[rows], grad[rows], k[:width], v[:width]
        scores = dot(qs, ks, NT) * SCALING
        keep = iota((half, width), 0) + part * half >= iota((half, width), 1)
        scores = jnp.where(keep, scores, -jnp.inf)
        raised = jnp.exp(scores - jnp.max(scores, axis=1, keepdims=True))
        probs = raised * (1.0 / jnp.sum(raised, axis=1, keepdims=True))
        rounded = probs.astype(BF16)
        out_ref[rows, :] = dot(rounded, vs)
        back = dot(gs, vs, NT)
        dscore = probs * (back - jnp.sum(back * probs, axis=1, keepdims=True)) * SCALING
        dround = dscore.astype(BF16)
        dq_ref[rows, :] = dot(dround, ks)
        grad_k.append(dot(dround, qs, TN))
        grad_v.append(dot(rounded, gs, TN))
    low = jnp.concatenate([grad_k[0] + grad_k[1][:half], grad_v[0] + grad_v[1][:half]], axis=1)
    high = jnp.concatenate([grad_k[1][half:], grad_v[1][half:]], axis=1)
    both = jnp.concatenate([low, high], axis=0).astype(BF16)
    total[...] += dot(x, both, TN)

    @pl.when(step == SEGS - 1)
    def _():
        me = lax.axis_index("dp")
        core = lax.rem(me, 2)
        for z in range(ZS):
            owner = lax.rem(me // 2 + z, ZS) * 2
            for part_ref, side in ((mine_ref, core), (other_ref, 1 - core)):
                at = pl.ds(pl.multiple_of((owner + side) * ROWS_OUT, ROWS_OUT), ROWS_OUT)
                part_ref[z] = total[at, :].astype(part_ref.dtype)


def local_part(tokens, w_query, w_key, w_value, cot, bias):
    seg = lambda width: pl.BlockSpec((SEG, width), lambda i: (i, 0))
    whole = pl.BlockSpec((D, DH), lambda i: (0, 0), pipeline_mode=pl.Buffered(1))
    fixed = pl.BlockSpec((ZS, ROWS_OUT, 2 * DH), lambda i: (0, 0, 0))
    return pl.pallas_call(
        local_kernel,
        grid=(SEGS,),
        out_shape=(
            jax.ShapeDtypeStruct((TOK, DH), BF16),
            jax.ShapeDtypeStruct((TOK, DH), F32),
            jax.ShapeDtypeStruct((TOK, DH), F32),
            jax.ShapeDtypeStruct((ZS, ROWS_OUT, 2 * DH), F32),
            jax.ShapeDtypeStruct((ZS, ROWS_OUT, 2 * DH), BF16),
        ),
        in_specs=[seg(D), whole, whole, whole, seg(DH), pl.BlockSpec(memory_space=pltpu.SMEM)],
        out_specs=(seg(DH), seg(DH), seg(DH), fixed, fixed),
        scratch_shapes=[pltpu.VMEM((D, 3 * DH), BF16), pltpu.VMEM((D, 2 * DH), F32)],
        compiler_params=pltpu.CompilerParams(
            dimension_semantics=("arbitrary",), vmem_limit_bytes=48 * MIB
        ),
        cost_estimate=pl.CostEstimate(
            flops=14_000_000_000, bytes_accessed=20 * MIB, transcendentals=1_600_000
        ),
        name="local",
    )(tokens, w_query, w_key, w_value, cot, bias)


CLASSES = ((2, 6), (4, 3), (8, 6))


def attend_all(members, tiles_n, refs):
    gate, tiles, queries_ref, cot_ref, outs, dqs = refs
    width = tiles_n * TILE
    at = [pl.ds(pl.multiple_of(block * QB, QB), QB) for block, _, _ in members]
    entries = [pl.ds(block * TOP, tiles_n) for block, _, _ in members]
    keys = [tiles[e, 0].reshape(width, DH) for e in entries]
    values = [tiles[e, 1].reshape(width, DH) for e in entries]
    up = [cot_ref[rows, :].astype(F32) for rows in at]
    queries = [queries_ref[rows, :] for rows in at]
    scores = [dot(k, q, NT) for k, q in zip(keys, queries)]
    back = [dot(v, (gate * u).astype(BF16), NT) for v, u in zip(values, up)]
    probs = []
    for s, (_, _, count) in zip(scores, members):
        s = jnp.where(iota((width, QB), 0) < count * TILE, s * SCALING, -jnp.inf)
        raised = jnp.exp(s - jnp.max(s, axis=0, keepdims=True))
        probs.append(raised * (1.0 / jnp.sum(raised, axis=0, keepdims=True)))
    out = [dot(p.astype(BF16), v, TN) for p, v in zip(probs, values)]
    dscore = [
        p * (b - jnp.sum(b * p, axis=0, keepdims=True)) * SCALING for p, b in zip(probs, back)
    ]
    dq = [dot(d.astype(BF16), k, TN) for d, k in zip(dscore, keys)]
    for rows, o, d in zip(at, out, dq):
        outs[rows, :] = o
        dqs[rows, :] = d


def memory_kernel(
    counts_ref, slot_ref, bias_ref, tiles_ref, queries_in, local_in, ldq_in, cot_in, tokens_ref,
    attended_out, mine_ref, other_ref, tiles, tokens, total, grads, gate_sum, lists, sizes,
    local_ref, ldq_ref, outs, dqs, queries_ref, cot_ref, attended_ref, sems, token_sems, row_sems,
    out_sems,
):
    pltpu.make_async_copy(queries_in, queries_ref, row_sems.at[2]).start()
    pltpu.make_async_copy(cot_in, cot_ref, row_sems.at[3]).start()

    def sort(block, _):
        count = counts_ref[0, block]

        def fetch(slot, _):
            entry = block * TOP + slot
            pltpu.make_async_copy(tiles_ref.at[slot_ref[0, entry]], tiles.at[entry], sems.at[entry]).start()
            return 0

        lax.fori_loop(0, count, fetch, 0)
        at = (count > 2).astype(jnp.int32) + (count > 4).astype(jnp.int32)
        place = sizes[at]
        lists[at, place] = block
        sizes[at] = place + 1

        def clear(slot, _):
            tiles[block * TOP + slot] = jnp.zeros((2, TILE, DH), BF16)
            return 0

        lax.fori_loop(count, lax.shift_left(2, at), clear, 0)
        return 0

    for at in range(len(CLASSES)):
        sizes[at] = 0
    lax.fori_loop(0, NQB, sort, 0)
    pltpu.make_async_copy(local_in, local_ref, row_sems.at[0]).start()
    pltpu.make_async_copy(ldq_in, ldq_ref, row_sems.at[1]).start()
    for part in range(SEGS):
        rows = pl.ds(part * SEG, SEG)
        pltpu.make_async_copy(tokens_ref.at[rows], tokens.at[rows], token_sems.at[part]).start()
    gate = gate_row(bias_ref)
    gate_sum[...] = jnp.zeros_like(gate_sum)
    pltpu.make_async_copy(queries_in, queries_ref, row_sems.at[2]).wait()
    pltpu.make_async_copy(cot_in, cot_ref, row_sems.at[3]).wait()
    for at, (tiles_n, group) in enumerate(CLASSES):

        def batch(i, _, at=at, tiles_n=tiles_n, group=group):
            members = []
            for k in range(group):
                valid = i * group + k < sizes[at]
                block = lists[at, jnp.minimum(i * group + k, sizes[at] - 1)]
                count = counts_ref[0, block]
                members.append((block, valid, count))

                def arrive(slot, _):
                    entry = block * TOP + slot
                    pltpu.make_async_copy(
                        tiles_ref.at[0], tiles.at[entry], sems.at[entry]
                    ).wait()
                    return 0

                lax.fori_loop(0, jnp.where(valid, count, 0), arrive, 0)
            attend_all(members, tiles_n, (gate, tiles, queries_ref, cot_ref, outs, dqs))
            return 0

        lax.fori_loop(0, pl.cdiv(sizes[at], group), batch, 0)
    pltpu.make_async_copy(local_in, local_ref, row_sems.at[0]).wait()
    pltpu.make_async_copy(ldq_in, ldq_ref, row_sems.at[1]).wait()
    for part in range(SEGS):
        rows = pl.ds(part * SEG, SEG)
        local = local_ref[rows, :]
        out = outs[rows, :]
        attended_ref[rows, :] = (gate * out + (1.0 - gate) * local).astype(BF16)
        pltpu.make_async_copy(attended_ref.at[rows], attended_out.at[rows], out_sems.at[part]).start()
        terms = cot_ref[rows, :].astype(F32) * (out - local)
        gate_sum[...] += jnp.sum(terms, axis=0, keepdims=True)
        grads[rows, :] = (dqs[rows, :] + ldq_ref[rows, :]).astype(BF16)
    for part in range(SEGS):
        rows = pl.ds(part * SEG, SEG)
        pltpu.make_async_copy(tokens_ref.at[rows], tokens.at[rows], token_sems.at[part]).wait()
        term = dot(grads[rows, :], tokens[rows, :], TN)
        if part == 0:
            total[...] = term
        else:
            total[...] += term
    me = lax.axis_index("dp")
    core = lax.rem(me, 2)
    extra = split_gate(gate_sum[...])
    for step in range(ZS):
        owner = lax.rem(me // 2 + step, ZS) * 2
        for out_ref, side in ((mine_ref, core), (other_ref, 1 - core)):
            cols = pl.ds(pl.multiple_of((owner + side) * ROWS_OUT, ROWS_OUT), ROWS_OUT)
            out_ref[step, :ROWS_OUT, :] = total[:, cols].T.astype(out_ref.dtype)
        mine_ref[step, ROWS_OUT:, :] = extra[0]
        other_ref[step, ROWS_OUT:, :] = extra[1].astype(BF16)
    for part in range(SEGS):
        rows = pl.ds(part * SEG, SEG)
        pltpu.make_async_copy(attended_ref.at[rows], attended_out.at[rows], out_sems.at[part]).wait()


def split_gate(term):
    high = term.astype(BF16).astype(F32)
    mid = (term - high).astype(BF16).astype(F32)
    low = term - high - mid
    at = iota((GATE_ROWS, DH), 0)
    spread = lambda row: jnp.broadcast_to(row, (GATE_ROWS, DH))
    parts = []
    for first in (0, 3):
        row = jnp.where(at == first, spread(high), jnp.where(at == first + 1, spread(mid), spread(low)))
        parts.append(jnp.where((at >= first) & (at < first + 3), row, 0.0))
    return parts


def memory_part(counts, slots, bias, tiles, queries, local, ldq, cot, tokens):
    smem = pl.BlockSpec(memory_space=pltpu.SMEM)
    vmem = pl.BlockSpec(memory_space=pltpu.VMEM)
    hbm = pl.BlockSpec(memory_space=pl.ANY)
    rows = ROWS_OUT + GATE_ROWS
    return pl.pallas_call(
        memory_kernel,
        out_shape=(
            jax.ShapeDtypeStruct((TOK, DH), BF16),
            jax.ShapeDtypeStruct((ZS, rows, DH), F32),
            jax.ShapeDtypeStruct((ZS, rows, DH), BF16),
        ),
        in_specs=[smem] * 3 + [hbm] * 6,
        out_specs=(hbm, vmem, vmem),
        scratch_shapes=[
            pltpu.VMEM((ENTRIES, 2, TILE, DH), BF16),
            pltpu.VMEM((TOK, D), BF16),
            pltpu.VMEM((DH, D), F32),
            pltpu.VMEM((TOK, DH), BF16),
            pltpu.VMEM((1, DH), F32),
            pltpu.SMEM((len(CLASSES), 32), jnp.int32),
            pltpu.SMEM((len(CLASSES),), jnp.int32),
            pltpu.VMEM((TOK, DH), F32),
            pltpu.VMEM((TOK, DH), F32),
            pltpu.VMEM((TOK, DH), F32),
            pltpu.VMEM((TOK, DH), F32),
            pltpu.VMEM((TOK, DH), BF16),
            pltpu.VMEM((TOK, DH), BF16),
            pltpu.VMEM((TOK, DH), BF16),
            pltpu.SemaphoreType.DMA((ENTRIES,)),
            pltpu.SemaphoreType.DMA((SEGS,)),
            pltpu.SemaphoreType.DMA((4,)),
            pltpu.SemaphoreType.DMA((SEGS,)),
        ],
        compiler_params=pltpu.CompilerParams(vmem_limit_bytes=59 * MIB),
        cost_estimate=pl.CostEstimate(
            flops=8_000_000_000, bytes_accessed=24 * MIB, transcendentals=1_600_000
        ),
        name="memory",
    )(counts, slots, bias, tiles, queries, local, ldq, cot, tokens)


def swap_cores(array):
    return lax.ppermute(array, "dp", [(i, i ^ 1) for i in range(2 * ZS)])


def along_z(array, step):
    return lax.ppermute(array, "dp", [(i, (i + 2 * step) % (2 * ZS)) for i in range(2 * ZS)])


def reduce_docs(mine, other):
    got = swap_cores(other)
    parts = [mine[0] + got[0].astype(F32)]
    for step in range(1, ZS):
        both = (mine[step] + got[step].astype(F32)).astype(BF16)
        parts.append(along_z(both, step).astype(F32))
    return parts


def exchange(array, axis):
    return lax.all_to_all(array, axis, split_axis=0, concat_axis=0, tiled=True)


def on_device(
    tokens,
    w_query,
    w_key,
    w_value,
    gate_bias,
    memory_keys,
    memory_values,
    retrieval_ids,
    retrieval_counts,
    cotangent,
):
    hidden = tokens[0]
    cot = cotangent[0]
    counts = retrieval_counts.reshape(1, NQB)
    table, slots = make_requests(retrieval_ids.reshape(NQB, TOP).T, counts)
    wanted = exchange(table, "mem")
    sent = serve(wanted, memory_keys[0], memory_values[0])
    hidden, sent = lax.optimization_barrier((hidden, sent))
    tiles = exchange(sent, "mem")
    queries, local, ldq, mine, other = local_part(hidden, w_query, w_key, w_value, cot, gate_bias)
    sum_kv = sum(reduce_docs(mine, other))
    share_k, share_v = sum_kv[:, :DH], sum_kv[:, DH:]
    counts, share_k, share_v = lax.optimization_barrier((counts, share_k, share_v))
    attended, mine, other = memory_part(
        counts, slots, gate_bias, tiles, queries, local, ldq, cot, hidden
    )
    parts = reduce_docs(mine, other)
    share_q = sum(part[:ROWS_OUT] for part in parts)
    gate_rows = sum(part[ROWS_OUT : ROWS_OUT + 6] for part in parts)
    gate = jax.nn.sigmoid(gate_bias)
    gate_total = jnp.sum(gate_rows) * gate * (1.0 - gate)
    return (attended[None], share_q, share_k, share_v, gate_total)


def solution(mesh):
    return jax.shard_map(
        on_device,
        mesh=mesh,
        in_specs=(
            P("dp", None, None),
            P(None, "mem"),
            P(None, "mem"),
            P(None, "mem"),
            P("mem"),
            P("dp", "mem", None),
            P("dp", "mem", None),
            P("dp", "mem", None, None),
            P("dp", "mem", None),
            P("dp", None, "mem"),
        ),
        out_specs=(P("dp", None, "mem"), P("dp", "mem"), P("dp", "mem"), P("dp", "mem"), P("mem")),
        check_vma=False,
    )
```
